32 devices in a mesh: dp: 2 (over core), ctx: 8 (over z, y), tp: 2 (over x).
Axes of the slice: x: 2, y: 2, z: 4, core: 2. Of those that a mesh axis runs over, the one named last changes fastest.
Arguments:
- prompt_states: bfloat16 [2048, 2048], P(('dp', 'ctx')), may hold values from -6 to 6
- continuation_states: bfloat16 [8192, 2048], P(('dp', 'ctx')), may hold values from -6 to 6
- continuation_offset: int32 [16], P(('dp', 'ctx')), may hold values from 0 to 511
- attention_gain: bfloat16 [2048], replicated, may hold values from 0.099609375 to 1.8984375
- query_weight: bfloat16 [2048, 1280], P(('dp', 'ctx'), 'tp'), may hold values from -0.125 to 0.125
- key_weight: bfloat16 [2048, 320], P(('dp', 'ctx')), may hold values from -0.125 to 0.125
- value_weight: bfloat16 [2048, 320], P(('dp', 'ctx')), may hold values from -0.125 to 0.125
- query_gain: bfloat16 [64], replicated, may hold values from 0.099609375 to 1.8984375
- key_gain: bfloat16 [64], replicated, may hold values from 0.099609375 to 1.8984375
- output_weight: bfloat16 [1280, 2048], P('tp', ('dp', 'ctx')), may hold values from -6 to 6
- feedforward_gain: bfloat16 [2048], replicated, may hold values from 0.099609375 to 1.8984375
- gate_weight: bfloat16 [2048, 5120], P(('dp', 'ctx'), 'tp'), may hold values from -0.125 to 0.125
- up_weight: bfloat16 [2048, 5120], P(('dp', 'ctx'), 'tp'), may hold values from -0.125 to 0.125
- down_weight: bfloat16 [5120, 2048], P('tp', ('dp', 'ctx')), may hold values from -0.078125 to 0.078125
- grad_prompt: bfloat16 [2048, 2048], P(('dp', 'ctx')), may hold values from -6 to 6
- grad_continuation: bfloat16 [8192, 2048], P(('dp', 'ctx')), may hold values from -6 to 6
Outputs:
- prompt_output: bfloat16 [2048, 2048], P(('dp', 'ctx'))
- continuation_output: bfloat16 [8192, 2048], P(('dp', 'ctx'))
- prompt_input_grad: bfloat16 [2048, 2048], P(('dp', 'ctx'))
- continuation_input_grad: bfloat16 [8192, 2048], P(('dp', 'ctx'))
- attention_gain_grad: float32 [2048], replicated
- query_weight_grad: float32 [2048, 1280], P(('dp', 'ctx'), 'tp')
- key_weight_grad: float32 [2048, 320], P(('dp', 'ctx'))
- value_weight_grad: float32 [2048, 320], P(('dp', 'ctx'))
- query_gain_grad: float32 [64], replicated
- key_gain_grad: float32 [64], replicated
- output_weight_grad: float32 [1280, 2048], P('tp', ('dp', 'ctx'))
- feedforward_gain_grad: float32 [2048], replicated
- gate_weight_grad: float32 [2048, 5120], P(('dp', 'ctx'), 'tp')
- up_weight_grad: float32 [2048, 5120], P(('dp', 'ctx'), 'tp')
- down_weight_grad: float32 [5120, 2048], P('tp', ('dp', 'ctx'))
The draws below stay inside these ranges and needn't reach their ends.
All inputs are finite; a program needn't handle non-finite values.
Results may differ from the reference program's by a relative error of at most 0.019.
Values may be sent and summed in bfloat16 or wider, within the bound.
No kernel may reach another device: no remote copies, remote signals or barrier semaphores. Data moves between devices by JAX's collectives and lax.ppermute only.
A program may use at most 256 MiB of HBM per device.

```python
import jax
import jax.numpy as jnp
from jax import lax

D = 2048
HEADS = 20
KVH = 5
HD = 64
FF = 5120
CL = 512
PROMPT = 1024
CONTS = 8
N_DP = 2


def set_ends(values, stream_key, low, largest):
    dims = values.shape
    place = [jax.random.randint(jax.random.fold_in(stream_key, axis), (), 0, dims[axis]) for axis in range(len(dims))]
    values = values.at[tuple(place)].set(low)
    longest = dims.index(max(dims))
    place[longest] = (place[longest] + 1) % dims[longest]
    return values.at[tuple(place)].set(largest)


def levels(key, extent, split, smallest, top_value):
    level = 1.0
    for dim, parts in split:
        draws = jax.random.uniform(jax.random.fold_in(jax.random.fold_in(key, 6), dim), (parts,), jnp.float32, smallest / len(split), top_value / len(split))
        level = level * jnp.repeat(jnp.exp(draws), extent[dim] // parts).reshape((-1,) + (1,) * (len(extent) - 1 - dim))
    return level


def normal_values(stream_key, extent, deviation, limit, split=(), kind=jnp.bfloat16):
    factor_of = levels(stream_key, extent, split, -0.22, 0.18) if split else 1.0
    values = jax.random.normal(stream_key, extent, jnp.float32) * deviation * factor_of
    return jnp.minimum(jnp.maximum(values, -limit), limit).astype(kind)


def setup_inputs(seed: int = 0) -> dict:
    splits = jax.random.split(jax.random.key(seed), 17)
    prompt_states = normal_values(splits[0], (N_DP * PROMPT, D), 1.0, 6.0, ((0, 16),))
    continuation_states = normal_values(splits[1], (N_DP * CONTS * CL, D), 1.0, 6.0, ((0, 16),))
    continuation_offset = set_ends(jax.random.randint(splits[2], (N_DP * CONTS,), 0, CL), jax.random.fold_in(splits[2], 1), 0, CL - 1).astype(jnp.int32)
    attention_gain = jnp.clip(1.0 + 0.18 * jax.random.normal(splits[3], (D,), jnp.float32), 0.099609375, 1.8984375).astype(jnp.bfloat16)
    query_weight = normal_values(splits[4], (D, HEADS * HD), D ** -0.5, 0.125, ((0, 16), (1, 2)))
    key_weight = normal_values(splits[5], (D, KVH * HD), D ** -0.5, 0.125, ((0, 16),))
    value_weight = normal_values(splits[6], (D, KVH * HD), D ** -0.5, 0.125, ((0, 16),))
    query_gain = jnp.clip(1.0 + 0.18 * jax.random.normal(splits[7], (HD,), jnp.float32), 0.099609375, 1.8984375).astype(jnp.bfloat16)
    key_gain = jnp.clip(1.0 + 0.18 * jax.random.normal(splits[8], (HD,), jnp.float32), 0.099609375, 1.8984375).astype(jnp.bfloat16)
    output_weight = normal_values(splits[9], (HEADS * HD, D), 1 ** -0.5, 6.0, ((0, 2), (1, 16)))
    feedforward_gain = jnp.clip(1.0 + 0.18 * jax.random.normal(splits[10], (D,), jnp.float32), 0.099609375, 1.8984375).astype(jnp.bfloat16)
    gate_weight = normal_values(splits[11], (D, FF), D ** -0.5, 0.125, ((0, 16), (1, 2)))
    up_weight = normal_values(splits[12], (D, FF), D ** -0.5, 0.125, ((0, 16), (1, 2)))
    down_weight = normal_values(splits[13], (FF, D), FF ** -0.5, 0.078125, ((0, 2), (1, 16)))
    grad_prompt = normal_values(splits[14], (N_DP * PROMPT, D), 1.0, 6.0, ((0, 16),))
    grad_continuation = normal_values(splits[15], (N_DP * CONTS * CL, D), 1.0, 6.0, ((0, 16),))
    return dict(prompt_states=prompt_states, continuation_states=continuation_states, continuation_offset=continuation_offset, attention_gain=attention_gain, query_weight=query_weight, key_weight=key_weight, value_weight=value_weight, query_gain=query_gain, key_gain=key_gain, output_weight=output_weight, feedforward_gain=feedforward_gain, gate_weight=gate_weight, up_weight=up_weight, down_weight=down_weight, grad_prompt=grad_prompt, grad_continuation=grad_continuation)


epsilon = 1e-06
highest = lax.Precision.HIGHEST

@jax.custom_vjp
def low(v):
    return lax.optimization_barrier(v.astype(jnp.bfloat16)).astype(jnp.float32)

@jax.custom_vjp
def low_back(v):
    return v

def low_keep(v):
    return (low(v), None)

def low_pass(kept, grad):
    return (grad,)

def back_keep(v):
    return (v, None)

def back_low(kept, grad):
    return (low(grad),)
low.defvjp(low_keep, low_pass)
low_back.defvjp(back_keep, back_low)

def matmul(multiplicand, multiplier):
    return jnp.dot(multiplicand, multiplier, precision=highest, preferred_element_type=jnp.float32)

def rms_norm(values, norm_gain):
    scale = lax.rsqrt(lax.optimization_barrier(jnp.mean(values * values, axis=-1, keepdims=True)) + epsilon)
    return values * scale * norm_gain

def rope_tables(positions, width):
    half_width = width // 2
    freqs = 10000.0 ** (-(2.0 * jnp.arange(half_width, dtype=jnp.float32)) / width)
    angles = positions[:, None] * freqs[None, :]
    angles = jnp.concatenate([angles, angles], axis=1)
    return (jnp.cos(angles), jnp.sin(angles))

def head_prep(raw_heads, norm_gain, cosine_table, sine_table):
    normed = rms_norm(raw_heads, norm_gain)
    half_width = raw_heads.shape[-1] // 2
    turned = jnp.concatenate([-normed[..., half_width:], normed[..., :half_width]], axis=-1)
    return normed * cosine_table[:, None, :] + turned * sine_table[:, None, :]

def attend(queries, key_rows, values, allowed):
    grouped = queries.reshape(queries.shape[0], KVH, HEADS // KVH, HD)
    scores = low_back(jnp.einsum('nkgd,mkd->kgnm', grouped, key_rows, precision=highest)) * 0.125
    scores = jnp.where(allowed, scores, -1e+30)
    row_max = lax.optimization_barrier(jnp.max(scores, axis=-1, keepdims=True))
    weights = jnp.exp(scores - row_max)
    probabilities = weights / lax.optimization_barrier(jnp.sum(weights, axis=-1, keepdims=True))
    combined = jnp.einsum('kgnm,mkd->nkgd', low(probabilities), values, precision=highest)
    return combined.reshape(queries.shape[0], HEADS * HD)

def layer(prompt_states, continuation_states, attention_gain, query_weight, key_weight, value_weight, query_gain, key_gain, output_weight, feedforward_gain, gate_weight, up_weight, down_weight, positions):
    inputs = jnp.concatenate([prompt_states, continuation_states], axis=0)
    normed = low(rms_norm(inputs, attention_gain))
    query_raw = low_back(matmul(normed, query_weight))
    key_raw = low_back(matmul(normed, key_weight))
    value_rows = low(low_back(matmul(normed, value_weight)))
    cosine_table, sine_table = rope_tables(positions, HD)
    query_rot = low(head_prep(query_raw.reshape(-1, HEADS, HD), query_gain, cosine_table, sine_table))
    key_rot = low(head_prep(key_raw.reshape(-1, KVH, HD), key_gain, cosine_table, sine_table))
    value_heads = value_rows.reshape(-1, KVH, HD)
    prompt_total = N_DP * PROMPT
    causal = jnp.arange(PROMPT)[:, None] >= jnp.arange(PROMPT)[None, :]
    causal_cont = jnp.arange(CL)[:, None] >= jnp.arange(CL)[None, :]
    allowed_cont = jnp.concatenate([jnp.ones((CL, PROMPT), dtype=bool), causal_cont], axis=1)
    prompt_parts = []
    cont_parts = []
    for group_index in range(N_DP):
        start = group_index * PROMPT
        prompt_query = query_rot[start:start + PROMPT]
        prompt_key = key_rot[start:start + PROMPT]
        prompt_value = value_heads[start:start + PROMPT]
        prompt_parts.append(jax.checkpoint(attend)(prompt_query, prompt_key, prompt_value, causal))
        cont_start = prompt_total + group_index * CONTS * CL
        cont_query = query_rot[cont_start:cont_start + CONTS * CL].reshape(CONTS, CL, HEADS, HD)
        cont_key = key_rot[cont_start:cont_start + CONTS * CL].reshape(CONTS, CL, KVH, HD)
        cont_value = value_heads[cont_start:cont_start + CONTS * CL].reshape(CONTS, CL, KVH, HD)

        def one_continuation(pieces, prompt_key=prompt_key, prompt_value=prompt_value):
            query_block, key_block, value_block = pieces
            return attend(query_block, jnp.concatenate([prompt_key, key_block], axis=0), jnp.concatenate([prompt_value, value_block], axis=0), allowed_cont)
        cont_out = lax.map(jax.checkpoint(one_continuation), (cont_query, cont_key, cont_value))
        cont_parts.append(cont_out.reshape(CONTS * CL, HEADS * HD))
    attended = low(low_back(jnp.concatenate(prompt_parts + cont_parts, axis=0)))
    resid = inputs + low_back(matmul(attended, output_weight))
    normed_two = low(rms_norm(resid, feedforward_gain))
    gate_rows = low_back(matmul(normed_two, gate_weight))
    up_rows = low_back(matmul(normed_two, up_weight))
    hidden = low(jax.nn.silu(gate_rows) * up_rows)
    output = resid + matmul(hidden, down_weight)
    return (output[:prompt_total], output[prompt_total:])

def reference(prompt_states, continuation_states, continuation_offset, attention_gain, query_weight, key_weight, value_weight, query_gain, key_gain, output_weight, feedforward_gain, gate_weight, up_weight, down_weight, grad_prompt, grad_continuation):
    prompt_pos = jnp.tile(jnp.arange(PROMPT, dtype=jnp.int32), N_DP)
    cont_pos = PROMPT + jnp.repeat(continuation_offset, CL) + jnp.tile(jnp.arange(CL, dtype=jnp.int32), N_DP * CONTS)
    positions = jnp.concatenate([prompt_pos, cont_pos], axis=0).astype(jnp.float32)
    floats = [array.astype(jnp.float32) for array in (prompt_states, continuation_states, attention_gain, query_weight, key_weight, value_weight, query_gain, key_gain, output_weight, feedforward_gain, gate_weight, up_weight, down_weight)]

    def layer_call(*params):
        return layer(*params, positions)
    outputs, pullback = jax.vjp(layer_call, *floats)
    gradients = pullback((grad_prompt.astype(jnp.float32), grad_continuation.astype(jnp.float32)))
    return (outputs[0].astype(jnp.bfloat16), outputs[1].astype(jnp.bfloat16), gradients[0].astype(jnp.bfloat16), gradients[1].astype(jnp.bfloat16), gradients[2], gradients[3], gradients[4], gradients[5], gradients[6], gradients[7], gradients[8], gradients[9], gradients[10], gradients[11], gradients[12])
```

```python
from functools import partial

import jax
import jax.numpy as jnp
from jax import lax
from jax.experimental import pallas as pl
from jax.experimental.pallas import tpu as pltpu
from jax.sharding import PartitionSpec as P

epsilon = 1e-06
bf16 = jnp.bfloat16
f32 = jnp.float32
lanes = 128


def params(megabytes=48):
    return pltpu.CompilerParams(vmem_limit_bytes=megabytes << 20)


def cost(flops, bytes_accessed, transcendentals=0):
    return pl.CostEstimate(
        flops=int(flops), bytes_accessed=int(bytes_accessed), transcendentals=int(transcendentals)
    )


def dot_nn(left, right):
    return jnp.dot(left, right, preferred_element_type=f32)


def dot_nt(left, right):
    return lax.dot_general(left, right, (((1,), (1,)), ((), ())), preferred_element_type=f32)


def dot_tn(left, right):
    return lax.dot_general(left, right, (((0,), (0,)), ((), ())), preferred_element_type=f32)


def half_mask(shape, size):
    return lax.broadcasted_iota(jnp.int32, shape, 1) % (2 * size) < size


def swap_quarters(values, head_size):
    quarter = head_size // 2
    low = half_mask(values.shape, quarter)
    return jnp.where(low, pltpu.roll(values, lanes - quarter, 1), pltpu.roll(values, quarter, 1))


def head_sums(values, low):
    first = jnp.sum(jnp.where(low, values, 0.0), axis=1, keepdims=True)
    second = jnp.sum(jnp.where(low, 0.0, values), axis=1, keepdims=True)
    return jnp.where(low, first, second)


def prep_kernel(raw_ref, cos_ref, sin_ref, gain_ref, out_ref, *, query_blocks, head_size, scale):
    block = pl.program_id(0)
    raw = raw_ref[...]
    low = half_mask(raw.shape, head_size)
    inverse = lax.rsqrt(head_sums(raw * raw, low) * (1.0 / head_size) + epsilon)
    normed = raw * inverse * gain_ref[0]
    rotated = normed * cos_ref[...] + swap_quarters(normed, head_size) * sin_ref[...]
    is_query = block < query_blocks
    rotated = rotated * jnp.where(is_query, scale, 1.0)
    out_ref[...] = jnp.where(jnp.logical_or(is_query, low), rotated, raw).astype(bf16)


def head_prep(raw, cos_table, sin_table, gains, query_blocks, head_size, scale):
    rows, width = raw.shape
    return pl.pallas_call(
        partial(prep_kernel, query_blocks=query_blocks, head_size=head_size, scale=scale),
        grid=(width // lanes,),
        in_specs=[
            pl.BlockSpec((rows, lanes), lambda i: (0, i)),
            pl.BlockSpec((rows, lanes), lambda i: (0, 0)),
            pl.BlockSpec((rows, lanes), lambda i: (0, 0)),
            pl.BlockSpec((1, 1, lanes), lambda i: (i, 0, 0)),
        ],
        out_specs=pl.BlockSpec((rows, lanes), lambda i: (0, i)),
        out_shape=jax.ShapeDtypeStruct((rows, width), bf16),
        compiler_params=params(),
        cost_estimate=cost(rows * width * 40, rows * width * 6),
        name="head_prep",
    )(raw, cos_table, sin_table, gains)


def prep_back_kernel(
    raw_ref, grad_ref, cos_ref, sin_ref, gain_ref, out_ref, gain_out_ref, *, has_value, head_size
):
    raw = raw_ref[...]
    grad = grad_ref[...]
    low = half_mask(raw.shape, head_size)
    turned = grad * cos_ref[...] + swap_quarters(grad * sin_ref[...], head_size)
    inverse = lax.rsqrt(head_sums(raw * raw, low) * (1.0 / head_size) + epsilon)
    normed = raw * inverse
    weighted = turned * gain_ref[0]
    mean = head_sums(weighted * normed, low) * (1.0 / head_size)
    result = inverse * (weighted - normed * mean)
    if has_value:
        result = jnp.where(low, result, grad)
    out_ref[...] = result.astype(bf16)
    gain_out_ref[0] = jnp.sum(turned * normed, axis=0, keepdims=True)


def head_prep_back(raw, raw_block, grad, cos_table, sin_table, gains, has_value, head_size):
    rows, width = grad.shape
    blocks = width // lanes
    return pl.pallas_call(
        partial(prep_back_kernel, has_value=has_value, head_size=head_size),
        grid=(blocks,),
        in_specs=[
            pl.BlockSpec((rows, lanes), lambda i: (0, i + raw_block)),
            pl.BlockSpec((rows, lanes), lambda i: (0, i)),
            pl.BlockSpec((rows, lanes), lambda i: (0, 0)),
            pl.BlockSpec((rows, lanes), lambda i: (0, 0)),
            pl.BlockSpec((1, 1, lanes), lambda i: (i + raw_block, 0, 0)),
        ],
        out_specs=[
            pl.BlockSpec((rows, lanes), lambda i: (0, i)),
            pl.BlockSpec((1, 1, lanes), lambda i: (i, 0, 0)),
        ],
        out_shape=[
            jax.ShapeDtypeStruct((rows, width), bf16),
            jax.ShapeDtypeStruct((blocks, 1, lanes), f32),
        ],
        compiler_params=params(),
        cost_estimate=cost(rows * width * 60, rows * width * 10),
        name="head_prep_back",
    )(raw, grad, cos_table, sin_table, gains)


def head_lanes(pair, index, head_size):
    values = pair.astype(f32)
    if index:
        values = pltpu.roll(values, head_size, 1)
    return jnp.where(half_mask(values.shape, head_size), values, 0.0)


def diagonal_mask(keys, rows):
    return lax.broadcasted_iota(jnp.int32, (keys, rows), 0) <= lax.broadcasted_iota(
        jnp.int32, (keys, rows), 1
    )


def attn_fwd_kernel(
    slot_ref, query_ref, keys_ref, mask_ref, out_ref, inverse_ref, acc, *, prompt_here, chunk, head_size
):
    rows = query_ref.shape[0]
    prompt_keys = mask_ref.shape[1]
    cont = rows - prompt_here
    half = cont // 2
    pair = query_ref[...]
    low = half_mask((1, lanes), head_size)
    results = []
    for index in range(2):
        query = head_lanes(pair, index, head_size).astype(bf16)

        def weigh(scores, keyvalue):
            ones_value = jnp.where(low, jnp.ones((), bf16), keyvalue)
            return dot_nn(jnp.exp(scores).astype(bf16), ones_value)

        keyvalue = keys_ref[0:prompt_keys]
        scores = dot_nt(query[:prompt_here], keyvalue)
        weights = (jnp.exp(scores) * mask_ref[...]).astype(bf16)
        acc[0:prompt_here] = dot_nn(weights, jnp.where(low, jnp.ones((), bf16), keyvalue))

        acc[prompt_here:rows] = jnp.zeros((cont, lanes), f32)
        cont_query = query[prompt_here:]

        def prompt_step(step, carry):
            piece = keys_ref[pl.ds(pl.multiple_of(step * chunk, chunk), chunk)]
            acc[prompt_here:rows] += weigh(dot_nt(cont_query, piece), piece)
            return carry

        lax.fori_loop(0, prompt_keys // chunk, prompt_step, 0)
        for block in range(2):
            start = prompt_here + block * half
            piece = keys_ref[prompt_keys + block * half : prompt_keys + (block + 1) * half]
            scores = dot_nt(query[start:], piece)
            row_ids = lax.broadcasted_iota(jnp.int32, scores.shape, 0)
            key_ids = lax.broadcasted_iota(jnp.int32, scores.shape, 1)
            acc[start:rows] += weigh(jnp.where(key_ids <= row_ids, scores, -1e30), piece)
        total = acc[...]
        results.append((total, pltpu.roll(total, head_size, 1)))
    first, first_moved = results[0]
    second, second_moved = results[1]
    full_low = half_mask((rows, lanes), head_size)
    inverse = 1.0 / jnp.where(full_low, first, second_moved)
    inverse_ref[...] = inverse
    out_ref[...] = (jnp.where(full_low, first_moved, second) * inverse).astype(bf16)


def attention_forward(slots, rotated, keys, prompt_mask, pairs, prompt_here, head_size):
    rows = rotated.shape[0]
    key_count = keys.shape[0]
    prompt_keys = prompt_mask.shape[1]
    chunk = min(512, prompt_keys)
    elements = 2 * pairs * rows * key_count
    return pl.pallas_call(
        partial(attn_fwd_kernel, prompt_here=prompt_here, chunk=chunk, head_size=head_size),
        grid_spec=pltpu.PrefetchScalarGridSpec(
            num_scalar_prefetch=1,
            grid=(pairs,),
            in_specs=[
                pl.BlockSpec((rows, lanes), lambda p, s: (0, p)),
                pl.BlockSpec((key_count, lanes), lambda p, s: (0, s[p])),
                pl.BlockSpec(prompt_mask.shape, lambda p, s: (0, 0)),
            ],
            out_specs=[
                pl.BlockSpec((rows, lanes), lambda p, s: (0, p)),
                pl.BlockSpec((rows, lanes), lambda p, s: (0, p)),
            ],
            scratch_shapes=[pltpu.VMEM((rows, lanes), f32)],
        ),
        out_shape=[
            jax.ShapeDtypeStruct((rows, pairs * lanes), bf16),
            jax.ShapeDtypeStruct((rows, pairs * lanes), f32),
        ],
        compiler_params=params(),
        cost_estimate=cost(elements * 1000, elements, elements),
        name="attention_forward",
    )(slots, rotated, keys, prompt_mask)


def attn_back_kernel(
    slot_ref,
    query_ref,
    keys_ref,
    mask_ref,
    attended_ref,
    inverse_ref,
    grad_ref,
    grad_query_ref,
    grad_keys_ref,
    q_sc,
    g_sc,
    d_sc,
    dq_sc,
    *,
    prompt_here,
    chunk,
    head_size,
):
    step_id = pl.program_id(0)
    rows = query_ref.shape[0]
    prompt_keys = mask_ref.shape[0]
    cont = rows - prompt_here
    half = cont // 2
    low = half_mask((1, lanes), head_size)
    full_low = half_mask((rows, lanes), head_size)
    lane_ids = lax.broadcasted_iota(jnp.int32, (rows, lanes), 1)

    fresh = jnp.logical_or(
        step_id == 0, slot_ref[step_id] != slot_ref[jnp.maximum(step_id - 1, 0)]
    )

    @pl.when(fresh)
    def _():
        grad_keys_ref[...] = jnp.zeros_like(grad_keys_ref)

    pair = query_ref[...]
    grad_pair = grad_ref[...].astype(f32)
    inverse = inverse_ref[...]
    product = grad_pair * attended_ref[...].astype(f32)
    delta = head_sums(product, full_low) * inverse
    scaled = grad_pair * inverse
    for index in range(2):
        grad_high = scaled if index else pltpu.roll(scaled, head_size, 1)
        delta_low = pltpu.roll(delta, head_size, 1) if index else delta
        delta_high_part = delta_low.astype(bf16).astype(f32)
        extra = jnp.where(
            lane_ids == 0, -delta_high_part, jnp.where(lane_ids == 1, delta_high_part - delta_low, 0.0)
        )
        q_sc[index] = head_lanes(pair, index, head_size).astype(bf16)
        g_sc[index] = jnp.where(full_low, 0.0, grad_high).astype(bf16)
        d_sc[index] = jnp.where(full_low, extra, grad_high).astype(bf16)
    dq_sc[...] = jnp.zeros_like(dq_sc)

    def block(key_start, key_size, row_start, row_stop, mask):
        piece = keys_ref[pl.ds(key_start, key_size)]
        ones_value = jnp.where(low, jnp.ones((), bf16), piece)
        count = row_stop - row_start

        def rows_of(ref):
            return jnp.concatenate([ref[0, row_start:row_stop], ref[1, row_start:row_stop]], axis=0)

        query = rows_of(q_sc)
        weights = jnp.exp(dot_nt(piece, query))
        if mask is not None:
            weights = mask(weights)
        grad_scores = (weights * dot_nt(ones_value, rows_of(d_sc))).astype(bf16)
        grad_keys_ref[pl.ds(key_start, key_size)] += dot_nn(grad_scores, query) + dot_nn(
            weights.astype(bf16), rows_of(g_sc)
        )
        grad_query = dot_tn(grad_scores, piece)
        dq_sc[0, row_start:row_stop] += grad_query[:count]
        dq_sc[1, row_start:row_stop] += grad_query[count:]

    def prompt_mask(weights):
        mask = mask_ref[...]
        return weights * jnp.concatenate([mask, mask], axis=1)

    block(0, prompt_keys, 0, prompt_here, prompt_mask)

    def prompt_step(step, carry):
        block(pl.multiple_of(step * chunk, chunk), chunk, prompt_here, rows, None)
        return carry

    lax.fori_loop(0, prompt_keys // chunk, prompt_step, 0)
    for part in range(2):
        start = prompt_here + part * half

        def causal(weights, size=rows - start):
            key_ids = lax.broadcasted_iota(jnp.int32, weights.shape, 0)
            row_ids = lax.broadcasted_iota(jnp.int32, weights.shape, 1)
            row_ids = jnp.where(row_ids < size, row_ids, row_ids - size)
            return jnp.where(key_ids <= row_ids, weights, 0.0)

        block(prompt_keys + part * half, half, start, rows, causal)
    moved = pltpu.roll(dq_sc[1], head_size, 1)
    grad_query_ref[...] = jnp.where(full_low, dq_sc[0], moved) * 0.125


def attention_backward(
    slots, rotated, keys, prompt_mask_t, attended, inverse, grad_attended, pairs, slot_count, prompt_here, head_size
):
    rows = rotated.shape[0]
    key_count = keys.shape[0]
    prompt_keys = prompt_mask_t.shape[0]
    chunk = min(512, prompt_keys)
    elements = 2 * pairs * rows * key_count
    pair_spec = pl.BlockSpec((rows, lanes), lambda p, s: (0, p))
    return pl.pallas_call(
        partial(attn_back_kernel, prompt_here=prompt_here, chunk=chunk, head_size=head_size),
        grid_spec=pltpu.PrefetchScalarGridSpec(
            num_scalar_prefetch=1,
            grid=(pairs,),
            in_specs=[
                pair_spec,
                pl.BlockSpec((key_count, lanes), lambda p, s: (0, s[p])),
                pl.BlockSpec(prompt_mask_t.shape, lambda p, s: (0, 0)),
                pair_spec,
                pair_spec,
                pair_spec,
            ],
            out_specs=[
                pair_spec,
                pl.BlockSpec((key_count, lanes), lambda p, s: (0, s[p])),
            ],
            scratch_shapes=[
                pltpu.VMEM((2, rows, lanes), bf16),
                pltpu.VMEM((2, rows, lanes), bf16),
                pltpu.VMEM((2, rows, lanes), bf16),
                pltpu.VMEM((2, rows, lanes), f32),
            ],
        ),
        out_shape=[
            jax.ShapeDtypeStruct((rows, pairs * lanes), f32),
            jax.ShapeDtypeStruct((key_count, slot_count * lanes), f32),
        ],
        compiler_params=params(),
        cost_estimate=cost(elements * 2500, elements, elements),
        name="attention_backward",
    )(slots, rotated, keys, prompt_mask_t, attended, inverse, grad_attended)


def ff_forward_kernel(rows_ref, gate_ref, up_ref, hidden_ref, gate_factor_ref, up_factor_ref):
    rows = rows_ref[...]
    gate = dot_nn(rows, gate_ref[...])
    up = dot_nn(rows, up_ref[...])
    sigmoid = 1.0 / (1.0 + jnp.exp(-gate))
    silu = gate * sigmoid
    hidden_ref[...] = (silu * up).astype(bf16)
    gate_factor_ref[...] = (up * sigmoid * (1.0 + gate * (1.0 - sigmoid))).astype(bf16)
    up_factor_ref[...] = silu.astype(bf16)


def ff_forward(rows, weights, units, tile=256):
    count, depth = rows.shape
    tiles = units // tile
    out = pl.BlockSpec((count, tile), lambda j: (0, j))
    return pl.pallas_call(
        ff_forward_kernel,
        grid=(tiles,),
        in_specs=[
            pl.BlockSpec((count, depth), lambda j: (0, 0)),
            pl.BlockSpec((depth, tile), lambda j: (0, j)),
            pl.BlockSpec((depth, tile), lambda j: (0, j + tiles)),
        ],
        out_specs=[out, out, out],
        out_shape=[jax.ShapeDtypeStruct((count, units), bf16)] * 3,
        compiler_params=params(),
        cost_estimate=cost(4 * count * depth * units, 4 * depth * units, count * units),
        name="ff_forward",
    )(rows, weights, weights)


def matmul_nt_kernel(left_ref, right_ref, out_ref):
    out_ref[...] = dot_nt(left_ref[...], right_ref[...]).astype(bf16)


def matmul_nt(left, weights, column_block, tile=256):
    count, depth = left.shape
    wide = weights.shape[0]
    return pl.pallas_call(
        matmul_nt_kernel,
        grid=(wide // tile,),
        in_specs=[
            pl.BlockSpec((count, depth), lambda j: (0, 0)),
            pl.BlockSpec((tile, depth), lambda j: (j, column_block)),
        ],
        out_specs=pl.BlockSpec((count, tile), lambda j: (0, j)),
        out_shape=jax.ShapeDtypeStruct((count, wide), bf16),
        compiler_params=params(),
        cost_estimate=cost(2 * count * depth * wide, 2 * depth * wide),
        name="matmul_nt",
    )(left, weights)


def ff_back_kernel(grad_ref, weight_ref, gate_factor_ref, up_factor_ref, gate_ref, up_ref):
    grad_hidden = dot_nn(grad_ref[...], weight_ref[...])
    gate_ref[...] = (grad_hidden * gate_factor_ref[...].astype(f32)).astype(bf16)
    up_ref[...] = (grad_hidden * up_factor_ref[...].astype(f32)).astype(bf16)


def ff_backward(grad_out, weights, gate_factor, up_factor, tile=256):
    count, depth = grad_out.shape
    units = gate_factor.shape[1]
    tiles = units // tile
    out = pl.BlockSpec((count, tile), lambda j: (0, j))
    return pl.pallas_call(
        ff_back_kernel,
        grid=(tiles,),
        in_specs=[
            pl.BlockSpec((count, depth), lambda j: (0, 0)),
            pl.BlockSpec((depth, tile), lambda j: (0, j + 2 * tiles)),
            out,
            out,
        ],
        out_specs=[out, out],
        out_shape=[jax.ShapeDtypeStruct((count, units), bf16)] * 2,
        compiler_params=params(),
        cost_estimate=cost(2 * count * depth * units, 2 * depth * units),
        name="ff_backward",
    )(grad_out, weights, gate_factor, up_factor)


def ff_input_kernel(gate_ref, up_ref, gate_weight_ref, up_weight_ref, out_ref):
    out_ref[...] = (
        dot_nt(gate_ref[...], gate_weight_ref[...]) + dot_nt(up_ref[...], up_weight_ref[...])
    ).astype(bf16)


def ff_input_grad(grad_gate, grad_up, weights, tile=256):
    count, units = grad_gate.shape
    wide = weights.shape[0]
    full = pl.BlockSpec((count, units), lambda j: (0, 0))
    return pl.pallas_call(
        ff_input_kernel,
        grid=(wide // tile,),
        in_specs=[
            full,
            full,
            pl.BlockSpec((tile, units), lambda j: (j, 0)),
            pl.BlockSpec((tile, units), lambda j: (j, 1)),
        ],
        out_specs=pl.BlockSpec((count, tile), lambda j: (0, j)),
        out_shape=jax.ShapeDtypeStruct((count, wide), bf16),
        compiler_params=params(),
        cost_estimate=cost(4 * count * units * wide, 4 * units * wide),
        name="ff_input_grad",
    )(grad_gate, grad_up, weights, weights)


def weight_grad_kernel(*refs, pieces, add):
    index_ref = refs[0]
    left = jnp.concatenate([ref[...] for ref in refs[1 : 1 + pieces]], axis=0)
    own_ref, other_ref = refs[1 + pieces : 3 + pieces]
    out_ref = refs[-1]
    right = jnp.concatenate([own_ref[...], other_ref[...]], axis=0)
    product = dot_nn(left, right)
    rows = left.shape[0] // pieces
    for piece in range(pieces):
        part = product[piece * rows : (piece + 1) * rows]
        if add:
            part = part + refs[-2][piece].astype(f32)
        out_ref[piece] = part.astype(bf16)


def weight_grad(indices, block, left_t, own, other, received=None):
    pieces = indices.shape[0]
    depth = left_t.shape[1]
    count, wide = own.shape
    tile = 512 if wide % 512 == 0 else 640 if wide % 640 == 0 else lanes
    out = pl.BlockSpec((pieces, block, tile), lambda j, s: (0, 0, j))
    in_specs = [
        pl.BlockSpec((block, depth), lambda j, s, piece=piece: (s[piece], 0)) for piece in range(pieces)
    ]
    in_specs += [pl.BlockSpec((count, tile), lambda j, s: (0, j))] * 2
    operands = [left_t] * pieces + [own, other]
    if received is not None:
        in_specs.append(out)
        operands.append(received)
    return pl.pallas_call(
        partial(weight_grad_kernel, pieces=pieces, add=received is not None),
        grid_spec=pltpu.PrefetchScalarGridSpec(
            num_scalar_prefetch=1,
            grid=(wide // tile,),
            in_specs=in_specs,
            out_specs=out,
        ),
        out_shape=jax.ShapeDtypeStruct((pieces, block, wide), bf16),
        compiler_params=params(),
        cost_estimate=cost(2 * pieces * block * depth * wide, 2 * (pieces * block + depth) * wide),
        name="weight_grad",
    )(indices, *operands)


def on_device(
    prompt_states,
    continuation_states,
    continuation_offset,
    attention_gain,
    query_weight,
    key_weight,
    value_weight,
    query_gain,
    key_gain,
    output_weight,
    feedforward_gain,
    gate_weight,
    up_weight,
    down_weight,
    grad_prompt,
    grad_continuation,
):
    ring = lax.axis_size("ctx")
    tensor_size = lax.axis_size("tp")
    zsize, ysize = ring // 2, 2
    prompt_here, width = prompt_states.shape
    cont_length = continuation_states.shape[0]
    rows_here = prompt_here + cont_length
    prompt_length = prompt_here * ring
    head_size = query_gain.shape[0]
    query_width = query_weight.shape[1]
    local_heads = query_width // head_size
    shared_heads = key_weight.shape[1] // head_size
    group_size = local_heads * tensor_size // shared_heads
    pairs = local_heads // 2
    units = gate_weight.shape[1]
    half_width = width // 2
    block = half_width // ring
    low_head = [t * local_heads // group_size for t in range(tensor_size)]
    slot_count = max(
        ((t + 1) * local_heads - 1) // group_size - low_head[t] + 1 for t in range(tensor_size)
    )

    data_rank = lax.axis_index("dp")
    context_rank = lax.axis_index("ctx")
    tensor_rank = lax.axis_index("tp")
    zrank, yrank = context_rank // ysize, context_rank % ysize
    first_shared = tensor_rank * local_heads // group_size

    def z_pass(values, shift):
        pairs_of = [
            (z * ysize + y, (z + shift) % zsize * ysize + y) for z in range(zsize) for y in range(ysize)
        ]
        return lax.ppermute(values, "ctx", pairs_of)

    def y_swap(values):
        return lax.ppermute(values, "ctx", [(i, i ^ 1) for i in range(ring)])

    def dp_swap(values):
        return lax.ppermute(values, "dp", [(0, 1), (1, 0)])

    def tp_swap(values):
        return lax.ppermute(values, "tp", [(0, 1), (1, 0)])

    def shared_slots(weight):
        return lax.dynamic_slice_in_dim(weight, first_shared * head_size, slot_count * head_size, 1).reshape(
            -1, slot_count, head_size
        )

    key_value_weight = jnp.concatenate(
        [shared_slots(key_weight), shared_slots(value_weight)], axis=2
    ).reshape(-1, slot_count * lanes)
    qkv_width = query_width + slot_count * lanes
    attn_weights = lax.all_gather(
        jnp.concatenate([query_weight, key_value_weight, output_weight.T], axis=1),
        ("dp", "ctx"),
        axis=0,
        tiled=True,
    )
    ff_weights = lax.all_gather(
        jnp.concatenate([gate_weight, up_weight, down_weight.T], axis=1),
        ("dp", "ctx"),
        axis=0,
        tiled=True,
    )
    qkv_weights = attn_weights[:, :qkv_width]
    out_weights_t = attn_weights[:, qkv_width:]

    row_ids = jnp.arange(rows_here, dtype=jnp.int32)
    positions = jnp.where(
        row_ids < prompt_here,
        context_rank * prompt_here + row_ids,
        prompt_length + continuation_offset[0] + row_ids - prompt_here,
    ).astype(f32)
    freqs = 10000.0 ** (-(2.0 * jnp.arange(head_size // 2, dtype=f32)) / head_size)
    angles = positions[:, None] * freqs[None, :]
    cosine, sine = jnp.cos(angles), jnp.sin(angles)
    cos_table = jnp.concatenate([cosine] * 4, axis=1)
    sin_table = jnp.concatenate([-sine, sine] * 2, axis=1)
    query_gain32, key_gain32 = query_gain.astype(f32), key_gain.astype(f32)
    gains = jnp.concatenate(
        [
            jnp.broadcast_to(jnp.concatenate([query_gain32] * 2), (pairs, 1, lanes)),
            jnp.broadcast_to(
                jnp.concatenate([key_gain32, jnp.ones((head_size,), f32)]), (slot_count, 1, lanes)
            ),
        ],
        axis=0,
    )
    steps = jnp.arange(zsize, dtype=jnp.int32)
    zs = (zrank + steps) % zsize
    own_blocks = zs * ysize + yrank
    other_blocks = zs * ysize + (1 - yrank)
    chunk_order = jnp.concatenate([own_blocks, other_blocks])
    key_places = jnp.repeat(chunk_order * prompt_here, prompt_here) + jnp.tile(
        jnp.arange(prompt_here, dtype=jnp.int32), ring
    )
    query_places = context_rank * prompt_here + jnp.arange(prompt_here, dtype=jnp.int32)
    prompt_mask = (key_places[None, :] <= query_places[:, None]).astype(f32)
    prompt_mask_t = (key_places[:, None] <= query_places[None, :]).astype(f32)
    slots = (
        (tensor_rank * local_heads + 2 * jnp.arange(pairs, dtype=jnp.int32)) // group_size - first_shared
    ).astype(jnp.int32)

    inputs = jnp.concatenate([prompt_states, continuation_states], axis=0).astype(f32)
    attn_gain32 = attention_gain.astype(f32)
    ff_gain32 = feedforward_gain.astype(f32)
    first_scale = lax.rsqrt(jnp.mean(inputs * inputs, axis=-1, keepdims=True) + epsilon)
    normed_low = (inputs * first_scale * attn_gain32).astype(bf16)
    raw = dot_nn(normed_low, qkv_weights)
    rotated = head_prep(raw, cos_table, sin_table, gains, pairs, head_size, 0.125)
    key_value = rotated[:, query_width:]
    own_chunk = key_value[:prompt_here]
    z_chunks = [own_chunk] + [z_pass(own_chunk, zsize - step) for step in range(1, zsize)]
    z_part = jnp.concatenate(z_chunks, axis=0)
    keys = jnp.concatenate([z_part, y_swap(z_part), key_value[prompt_here:]], axis=0)
    attended, inverse = attention_forward(
        slots, rotated, keys, prompt_mask, pairs, prompt_here, head_size
    )
    attn_part = dot_nt(attended, out_weights_t).astype(bf16)
    resid = inputs + (attn_part.astype(f32) + tp_swap(attn_part).astype(f32))
    second_scale = lax.rsqrt(jnp.mean(resid * resid, axis=-1, keepdims=True) + epsilon)
    second_normed = resid * second_scale
    normed_two = (second_normed * ff_gain32).astype(bf16)
    hidden, gate_factor, up_factor = ff_forward(normed_two, ff_weights, units)
    ff_part = matmul_nt(hidden, ff_weights, 2)
    output = (resid + (ff_part.astype(f32) + tp_swap(ff_part).astype(f32))).astype(bf16)

    def columns_of(values, rank):
        return lax.dynamic_slice_in_dim(values, rank * half_width, half_width, 1)

    def both_rows_t(values):
        received = dp_swap(columns_of(values, 1 - data_rank))
        return jnp.concatenate([columns_of(values, data_rank), received], axis=0).T

    def reduced(left_t, own):
        other = dp_swap(own)
        sent = y_swap(weight_grad(other_blocks, block, left_t, own, other))
        kept = weight_grad(own_blocks, block, left_t, own, other, sent)
        total = kept[0].astype(f32)
        for step in range(1, zsize):
            total = total + z_pass(kept[step], step).astype(f32)
        return total

    grad_out = jnp.concatenate([grad_prompt, grad_continuation], axis=0)
    grad_out_t = both_rows_t(grad_out)
    down_done = reduced(grad_out_t, hidden).T

    grad_gate, grad_up = ff_backward(grad_out, ff_weights, gate_factor, up_factor)
    normed_two_t = both_rows_t(normed_two)
    gate_done = reduced(normed_two_t, grad_gate)
    up_done = reduced(normed_two_t, grad_up)
    grad_part = ff_input_grad(grad_gate, grad_up, ff_weights)
    grad_normed_two = grad_part.astype(f32) + tp_swap(grad_part).astype(f32)

    def norm_back(grad_rows, normed_rows, scale, gain):
        weighted = grad_rows * gain
        mean = jnp.mean(weighted * normed_rows, axis=-1, keepdims=True)
        return scale * (weighted - normed_rows * mean), jnp.sum(grad_rows * normed_rows, axis=0)

    grad_resid_part, grad_ff_gain = norm_back(grad_normed_two, second_normed, second_scale, ff_gain32)
    grad_resid = grad_out.astype(f32) + grad_resid_part
    grad_resid_low = grad_resid.astype(bf16)
    grad_attended = dot_nn(grad_resid_low, out_weights_t).astype(bf16)
    out_done = reduced(both_rows_t(grad_resid_low), attended).T

    grad_query, grad_keys = attention_backward(
        slots,
        rotated,
        keys,
        prompt_mask_t,
        attended,
        inverse,
        grad_attended,
        pairs,
        slot_count,
        prompt_here,
        head_size,
    )
    grad_keys_prompt = grad_keys[:prompt_length].astype(bf16)
    half_prompt = prompt_length // 2
    kept_keys = grad_keys_prompt[:half_prompt].astype(f32) + y_swap(grad_keys_prompt[half_prompt:]).astype(f32)
    kept_keys = kept_keys.astype(bf16)
    own_keys = kept_keys[:prompt_here].astype(f32)
    for step in range(1, zsize):
        own_keys = own_keys + z_pass(
            kept_keys[step * prompt_here : (step + 1) * prompt_here], step
        ).astype(f32)
    grad_key_value = jnp.concatenate([own_keys, grad_keys[prompt_length:]], axis=0)
    grad_query_low, query_gain_parts = head_prep_back(
        raw, 0, grad_query, cos_table, sin_table, gains, False, head_size
    )
    grad_shared_low, key_gain_parts = head_prep_back(
        raw, pairs, grad_key_value, cos_table, sin_table, gains, True, head_size
    )
    grad_qkv = jnp.concatenate([grad_query_low, grad_shared_low], axis=1)
    qkv_done = reduced(both_rows_t(normed_low), grad_qkv)
    qkv_part = dot_nt(grad_qkv, qkv_weights).astype(bf16)
    grad_normed = qkv_part.astype(f32) + tp_swap(qkv_part).astype(f32)
    grad_input_part, grad_attn_gain = norm_back(grad_normed, inputs * first_scale, first_scale, attn_gain32)
    grad_input = (grad_resid + grad_input_part).astype(bf16)

    shared_done = qkv_done[:, query_width:]
    shared_other = tp_swap(shared_done)
    from_first = jnp.where(tensor_rank == 0, shared_done, shared_other)
    from_second = jnp.where(tensor_rank == 0, shared_other, shared_done)

    def all_heads(values, offset, which):
        block = values.reshape(-1, slot_count, 2, head_size)[:, :, which].reshape(-1, slot_count * head_size)
        before = offset * head_size
        after = shared_heads * head_size - before - slot_count * head_size
        return jnp.pad(block, ((0, 0), (before, after)))

    key_done, value_done = (
        all_heads(from_first, low_head[0], which) + all_heads(from_second, low_head[1], which)
        for which in range(2)
    )

    query_gain_sum = jnp.sum(query_gain_parts.reshape(-1, head_size), axis=0)
    key_gain_sum = jnp.sum(key_gain_parts[:, 0, :head_size], axis=0)
    head_gains = jnp.concatenate([query_gain_sum, key_gain_sum])
    head_gains = head_gains + tp_swap(head_gains)
    gain_sums = jnp.concatenate([grad_attn_gain, grad_ff_gain, head_gains]).reshape(-1, lanes)
    gain_sums = gain_sums + dp_swap(gain_sums)
    gain_sums = gain_sums + y_swap(gain_sums)
    gain_total = gain_sums
    for step in range(1, zsize):
        gain_total = gain_total + z_pass(gain_sums, step)
    gain_total = gain_total.reshape(-1)
    return (
        output[:prompt_here],
        output[prompt_here:],
        grad_input[:prompt_here],
        grad_input[prompt_here:],
        gain_total[:width],
        qkv_done[:, :query_width],
        key_done,
        value_done,
        gain_total[2 * width : 2 * width + head_size],
        gain_total[2 * width + head_size :],
        out_done,
        gain_total[width : 2 * width],
        gate_done,
        up_done,
        down_done,
    )


def solution(mesh):
    in_specs = (
        P(("dp", "ctx"), None),
        P(("dp", "ctx"), None),
        P(("dp", "ctx")),
        P(),
        P(("dp", "ctx"), "tp"),
        P(("dp", "ctx"), None),
        P(("dp", "ctx"), None),
        P(),
        P(),
        P("tp", ("dp", "ctx")),
        P(),
        P(("dp", "ctx"), "tp"),
        P(("dp", "ctx"), "tp"),
        P("tp", ("dp", "ctx")),
        P(("dp", "ctx"), None),
        P(("dp", "ctx"), None),
    )
    out_specs = (
        P(("dp", "ctx"), None),
        P(("dp", "ctx"), None),
        P(("dp", "ctx"), None),
        P(("dp", "ctx"), None),
        P(),
        P(("dp", "ctx"), "tp"),
        P(("dp", "ctx"), None),
        P(("dp", "ctx"), None),
        P(),
        P(),
        P("tp", ("dp", "ctx")),
        P(),
        P(("dp", "ctx"), "tp"),
        P(("dp", "ctx"), "tp"),
        P("tp", ("dp", "ctx")),
    )
    return jax.shard_map(
        on_device, mesh=mesh, in_specs=in_specs, out_specs=out_specs, check_vma=False
    )
```

```python
from functools import partial

import jax
import jax.numpy as jnp
from jax import lax
from jax.experimental import pallas as pl
from jax.experimental.pallas import tpu as pltpu
from jax.sharding import PartitionSpec as P

epsilon = 1e-06
bf16 = jnp.bfloat16
f32 = jnp.float32
lanes = 128


def params(megabytes=48):
    return pltpu.CompilerParams(vmem_limit_bytes=megabytes << 20)


def cost(flops, bytes_accessed, transcendentals=0):
    return pl.CostEstimate(
        flops=int(flops) * 8, bytes_accessed=int(bytes_accessed) * 8, transcendentals=int(transcendentals) * 8
    )


def dot_nn(left, right):
    return jnp.dot(left, right, preferred_element_type=f32)


def dot_nt(left, right):
    return lax.dot_general(left, right, (((1,), (1,)), ((), ())), preferred_element_type=f32)


def dot_tn(left, right):
    return lax.dot_general(left, right, (((0,), (0,)), ((), ())), preferred_element_type=f32)


def half_mask(shape, size):
    return lax.broadcasted_iota(jnp.int32, shape, 1) % (2 * size) < size


def swap_quarters(values, head_size):
    quarter = head_size // 2
    low = half_mask(values.shape, quarter)
    return jnp.where(low, pltpu.roll(values, lanes - quarter, 1), pltpu.roll(values, quarter, 1))


def head_sums(values, low):
    first = jnp.sum(jnp.where(low, values, 0.0), axis=1, keepdims=True)
    second = jnp.sum(jnp.where(low, 0.0, values), axis=1, keepdims=True)
    return jnp.where(low, first, second)


def prep_kernel(raw_ref, cos_ref, sin_ref, gain_ref, out_ref, *, query_blocks, head_size, scale):
    block = pl.program_id(0)
    raw = raw_ref[...]
    low = half_mask(raw.shape, head_size)
    inverse = lax.rsqrt(head_sums(raw * raw, low) * (1.0 / head_size) + epsilon)
    normed = raw * inverse * gain_ref[0]
    rotated = normed * cos_ref[...] + swap_quarters(normed, head_size) * sin_ref[...]
    is_query = block < query_blocks
    rotated = rotated * jnp.where(is_query, scale, 1.0)
    out_ref[...] = jnp.where(jnp.logical_or(is_query, low), rotated, raw).astype(bf16)


def head_prep(raw, cos_table, sin_table, gains, query_blocks, head_size, scale):
    rows, width = raw.shape
    return pl.pallas_call(
        partial(prep_kernel, query_blocks=query_blocks, head_size=head_size, scale=scale),
        grid=(width // lanes,),
        in_specs=[
            pl.BlockSpec((rows, lanes), lambda i: (0, i)),
            pl.BlockSpec((rows, lanes), lambda i: (0, 0)),
            pl.BlockSpec((rows, lanes), lambda i: (0, 0)),
            pl.BlockSpec((1, 1, lanes), lambda i: (i, 0, 0)),
        ],
        out_specs=pl.BlockSpec((rows, lanes), lambda i: (0, i)),
        out_shape=jax.ShapeDtypeStruct((rows, width), bf16),
        compiler_params=params(),
        cost_estimate=cost(rows * width * 40, rows * width * 6),
        name="head_prep",
    )(raw, cos_table, sin_table, gains)


def prep_back_kernel(
    raw_ref, grad_ref, cos_ref, sin_ref, gain_ref, out_ref, gain_out_ref, *, has_value, head_size
):
    raw = raw_ref[...]
    grad = grad_ref[...]
    low = half_mask(raw.shape, head_size)
    turned = grad * cos_ref[...] + swap_quarters(grad * sin_ref[...], head_size)
    inverse = lax.rsqrt(head_sums(raw * raw, low) * (1.0 / head_size) + epsilon)
    normed = raw * inverse
    weighted = turned * gain_ref[0]
    mean = head_sums(weighted * normed, low) * (1.0 / head_size)
    result = inverse * (weighted - normed * mean)
    if has_value:
        result = jnp.where(low, result, grad)
    out_ref[...] = result.astype(bf16)
    gain_out_ref[0] = jnp.sum(turned * normed, axis=0, keepdims=True)


def head_prep_back(raw, raw_block, grad, cos_table, sin_table, gains, has_value, head_size):
    rows, width = grad.shape
    blocks = width // lanes
    return pl.pallas_call(
        partial(prep_back_kernel, has_value=has_value, head_size=head_size),
        grid=(blocks,),
        in_specs=[
            pl.BlockSpec((rows, lanes), lambda i: (0, i + raw_block)),
            pl.BlockSpec((rows, lanes), lambda i: (0, i)),
            pl.BlockSpec((rows, lanes), lambda i: (0, 0)),
            pl.BlockSpec((rows, lanes), lambda i: (0, 0)),
            pl.BlockSpec((1, 1, lanes), lambda i: (i + raw_block, 0, 0)),
        ],
        out_specs=[
            pl.BlockSpec((rows, lanes), lambda i: (0, i)),
            pl.BlockSpec((1, 1, lanes), lambda i: (i, 0, 0)),
        ],
        out_shape=[
            jax.ShapeDtypeStruct((rows, width), bf16),
            jax.ShapeDtypeStruct((blocks, 1, lanes), f32),
        ],
        compiler_params=params(),
        cost_estimate=cost(rows * width * 60, rows * width * 10),
        name="head_prep_back",
    )(raw, grad, cos_table, sin_table, gains)


def head_lanes(pair, index, head_size):
    values = pair.astype(f32)
    if index:
        values = pltpu.roll(values, head_size, 1)
    return jnp.where(half_mask(values.shape, head_size), values, 0.0)


def diagonal_mask(keys, rows):
    return lax.broadcasted_iota(jnp.int32, (keys, rows), 0) <= lax.broadcasted_iota(
        jnp.int32, (keys, rows), 1
    )


def attn_fwd_kernel(
    slot_ref, query_ref, keys_ref, mask_ref, out_ref, inverse_ref, acc, *, prompt_here, chunk, head_size
):
    rows = query_ref.shape[0]
    prompt_keys = mask_ref.shape[1]
    cont = rows - prompt_here
    half = cont // 2
    pair = query_ref[...]
    low = half_mask((1, lanes), head_size)
    results = []
    for index in range(2):
        query = head_lanes(pair, index, head_size).astype(bf16)

        def weigh(scores, keyvalue):
            ones_value = jnp.where(low, jnp.ones((), bf16), keyvalue)
            return dot_nn(jnp.exp(scores).astype(bf16), ones_value)

        keyvalue = keys_ref[0:prompt_keys]
        scores = dot_nt(query[:prompt_here], keyvalue)
        weights = (jnp.exp(scores) * mask_ref[...]).astype(bf16)
        acc[0:prompt_here] = dot_nn(weights, jnp.where(low, jnp.ones((), bf16), keyvalue))

        acc[prompt_here:rows] = jnp.zeros((cont, lanes), f32)
        cont_query = query[prompt_here:]

        def prompt_step(step, carry):
            piece = keys_ref[pl.ds(pl.multiple_of(step * chunk, chunk), chunk)]
            acc[prompt_here:rows] += weigh(dot_nt(cont_query, piece), piece)
            return carry

        lax.fori_loop(0, prompt_keys // chunk, prompt_step, 0)
        for block in range(2):
            start = prompt_here + block * half
            piece = keys_ref[prompt_keys + block * half : prompt_keys + (block + 1) * half]
            scores = dot_nt(query[start:], piece)
            row_ids = lax.broadcasted_iota(jnp.int32, scores.shape, 0)
            key_ids = lax.broadcasted_iota(jnp.int32, scores.shape, 1)
            acc[start:rows] += weigh(jnp.where(key_ids <= row_ids, scores, -1e30), piece)
        total = acc[...]
        results.append((total, pltpu.roll(total, head_size, 1)))
    first, first_moved = results[0]
    second, second_moved = results[1]
    full_low = half_mask((rows, lanes), head_size)
    inverse = 1.0 / jnp.where(full_low, first, second_moved)
    inverse_ref[...] = inverse
    out_ref[...] = (jnp.where(full_low, first_moved, second) * inverse).astype(bf16)


def attention_forward(slots, rotated, keys, prompt_mask, pairs, prompt_here, head_size):
    rows = rotated.shape[0]
    key_count = keys.shape[0]
    prompt_keys = prompt_mask.shape[1]
    chunk = min(512, prompt_keys)
    elements = 2 * pairs * rows * key_count
    return pl.pallas_call(
        partial(attn_fwd_kernel, prompt_here=prompt_here, chunk=chunk, head_size=head_size),
        grid_spec=pltpu.PrefetchScalarGridSpec(
            num_scalar_prefetch=1,
            grid=(pairs,),
            in_specs=[
                pl.BlockSpec((rows, lanes), lambda p, s: (0, p)),
                pl.BlockSpec((key_count, lanes), lambda p, s: (0, s[p])),
                pl.BlockSpec(prompt_mask.shape, lambda p, s: (0, 0)),
            ],
            out_specs=[
                pl.BlockSpec((rows, lanes), lambda p, s: (0, p)),
                pl.BlockSpec((rows, lanes), lambda p, s: (0, p)),
            ],
            scratch_shapes=[pltpu.VMEM((rows, lanes), f32)],
        ),
        out_shape=[
            jax.ShapeDtypeStruct((rows, pairs * lanes), bf16),
            jax.ShapeDtypeStruct((rows, pairs * lanes), f32),
        ],
        compiler_params=params(),
        cost_estimate=cost(elements * 1000, elements, elements),
        name="attention_forward",
    )(slots, rotated, keys, prompt_mask)


def attn_back_kernel(
    slot_ref,
    query_ref,
    keys_ref,
    mask_ref,
    attended_ref,
    inverse_ref,
    grad_ref,
    grad_query_ref,
    grad_keys_ref,
    q_sc,
    g_sc,
    d_sc,
    dq_sc,
    *,
    prompt_here,
    chunk,
    head_size,
):
    step_id = pl.program_id(0)
    rows = query_ref.shape[0]
    prompt_keys = mask_ref.shape[0]
    cont = rows - prompt_here
    half = cont // 2
    low = half_mask((1, lanes), head_size)
    full_low = half_mask((rows, lanes), head_size)
    lane_ids = lax.broadcasted_iota(jnp.int32, (rows, lanes), 1)

    fresh = jnp.logical_or(
        step_id == 0, slot_ref[step_id] != slot_ref[jnp.maximum(step_id - 1, 0)]
    )

    @pl.when(fresh)
    def _():
        grad_keys_ref[...] = jnp.zeros_like(grad_keys_ref)

    pair = query_ref[...]
    grad_pair = grad_ref[...].astype(f32)
    inverse = inverse_ref[...]
    product = grad_pair * attended_ref[...].astype(f32)
    delta = head_sums(product, full_low) * inverse
    scaled = grad_pair * inverse
    for index in range(2):
        grad_high = scaled if index else pltpu.roll(scaled, head_size, 1)
        delta_low = pltpu.roll(delta, head_size, 1) if index else delta
        delta_high_part = delta_low.astype(bf16).astype(f32)
        extra = jnp.where(
            lane_ids == 0, -delta_high_part, jnp.where(lane_ids == 1, delta_high_part - delta_low, 0.0)
        )
        q_sc[index] = head_lanes(pair, index, head_size).astype(bf16)
        g_sc[index] = jnp.where(full_low, 0.0, grad_high).astype(bf16)
        d_sc[index] = jnp.where(full_low, extra, grad_high).astype(bf16)
    dq_sc[...] = jnp.zeros_like(dq_sc)

    def block(key_start, key_size, row_start, row_stop, mask):
        piece = keys_ref[pl.ds(key_start, key_size)]
        ones_value = jnp.where(low, jnp.ones((), bf16), piece)
        count = row_stop - row_start

        def rows_of(ref):
            return jnp.concatenate([ref[0, row_start:row_stop], ref[1, row_start:row_stop]], axis=0)

        query = rows_of(q_sc)
        weights = jnp.exp(dot_nt(piece, query))
        if mask is not None:
            weights = mask(weights)
        grad_scores = (weights * dot_nt(ones_value, rows_of(d_sc))).astype(bf16)
        grad_keys_ref[pl.ds(key_start, key_size)] += dot_nn(grad_scores, query) + dot_nn(
            weights.astype(bf16), rows_of(g_sc)
        )
        grad_query = dot_tn(grad_scores, piece)
        dq_sc[0, row_start:row_stop] += grad_query[:count]
        dq_sc[1, row_start:row_stop] += grad_query[count:]

    def prompt_mask(weights):
        mask = mask_ref[...]
        return weights * jnp.concatenate([mask, mask], axis=1)

    block(0, prompt_keys, 0, prompt_here, prompt_mask)

    def prompt_step(step, carry):
        block(pl.multiple_of(step * chunk, chunk), chunk, prompt_here, rows, None)
        return carry

    lax.fori_loop(0, prompt_keys // chunk, prompt_step, 0)
    for part in range(2):
        start = prompt_here + part * half

        def causal(weights, size=rows - start):
            key_ids = lax.broadcasted_iota(jnp.int32, weights.shape, 0)
            row_ids = lax.broadcasted_iota(jnp.int32, weights.shape, 1)
            row_ids = jnp.where(row_ids < size, row_ids, row_ids - size)
            return jnp.where(key_ids <= row_ids, weights, 0.0)

        block(prompt_keys + part * half, half, start, rows, causal)
    moved = pltpu.roll(dq_sc[1], head_size, 1)
    grad_query_ref[...] = jnp.where(full_low, dq_sc[0], moved) * 0.125


def attention_backward(
    slots, rotated, keys, prompt_mask_t, attended, inverse, grad_attended, pairs, slot_count, prompt_here, head_size
):
    rows = rotated.shape[0]
    key_count = keys.shape[0]
    prompt_keys = prompt_mask_t.shape[0]
    chunk = min(512, prompt_keys)
    elements = 2 * pairs * rows * key_count
    pair_spec = pl.BlockSpec((rows, lanes), lambda p, s: (0, p))
    return pl.pallas_call(
        partial(attn_back_kernel, prompt_here=prompt_here, chunk=chunk, head_size=head_size),
        grid_spec=pltpu.PrefetchScalarGridSpec(
            num_scalar_prefetch=1,
            grid=(pairs,),
            in_specs=[
                pair_spec,
                pl.BlockSpec((key_count, lanes), lambda p, s: (0, s[p])),
                pl.BlockSpec(prompt_mask_t.shape, lambda p, s: (0, 0)),
                pair_spec,
                pair_spec,
                pair_spec,
            ],
            out_specs=[
                pair_spec,
                pl.BlockSpec((key_count, lanes), lambda p, s: (0, s[p])),
            ],
            scratch_shapes=[
                pltpu.VMEM((2, rows, lanes), bf16),
                pltpu.VMEM((2, rows, lanes), bf16),
                pltpu.VMEM((2, rows, lanes), bf16),
                pltpu.VMEM((2, rows, lanes), f32),
            ],
        ),
        out_shape=[
            jax.ShapeDtypeStruct((rows, pairs * lanes), f32),
            jax.ShapeDtypeStruct((key_count, slot_count * lanes), f32),
        ],
        compiler_params=params(),
        cost_estimate=cost(elements * 2500, elements, elements),
        name="attention_backward",
    )(slots, rotated, keys, prompt_mask_t, attended, inverse, grad_attended)


ff_tile = 256


def ff_forward_kernel(rows_ref, weight_ref, hidden_ref, gate_factor_ref, up_factor_ref):
    both = dot_nn(rows_ref[...], weight_ref[...])
    gate, up = both[:, :ff_tile], both[:, ff_tile:]
    sigmoid = 1.0 / (1.0 + jnp.exp(-gate))
    silu = gate * sigmoid
    hidden_ref[...] = (silu * up).astype(bf16)
    gate_factor_ref[...] = (up * sigmoid * (1.0 + gate * (1.0 - sigmoid))).astype(bf16)
    up_factor_ref[...] = silu.astype(bf16)


def ff_forward(rows, weights, units):
    count, depth = rows.shape
    out = pl.BlockSpec((count, ff_tile), lambda j: (0, j))
    return pl.pallas_call(
        ff_forward_kernel,
        grid=(units // ff_tile,),
        in_specs=[
            pl.BlockSpec((count, depth), lambda j: (0, 0)),
            pl.BlockSpec((depth, 2 * ff_tile), lambda j: (0, j)),
        ],
        out_specs=[out, out, out],
        out_shape=[jax.ShapeDtypeStruct((count, units), bf16)] * 3,
        compiler_params=params(),
        cost_estimate=cost(4 * count * depth * units, 4 * depth * units, count * units),
        name="ff_forward",
    )(rows, weights)


def matmul_nt_kernel(left_ref, right_ref, out_ref):
    out_ref[...] = dot_nt(left_ref[...], right_ref[...]).astype(bf16)


def matmul_nt(left, weights, column_block, first=0, wide=None, tile=256):
    count, depth = left.shape
    wide = wide or weights.shape[0]
    return pl.pallas_call(
        matmul_nt_kernel,
        grid=(wide // tile,),
        in_specs=[
            pl.BlockSpec((count, depth), lambda j: (0, 0)),
            pl.BlockSpec((tile, depth), lambda j: (j + first // tile, column_block)),
        ],
        out_specs=pl.BlockSpec((count, tile), lambda j: (0, j)),
        out_shape=jax.ShapeDtypeStruct((count, wide), bf16),
        compiler_params=params(),
        cost_estimate=cost(2 * count * depth * wide, 2 * depth * wide),
        name="matmul_nt",
    )(left, weights)


def split_tiles_kernel(both_ref, gate_ref, up_ref):
    gate_ref[...] = both_ref[:, :ff_tile].astype(f32)
    up_ref[...] = both_ref[:, ff_tile:].astype(f32)


def split_tiles(both):
    rows, wide = both.shape
    out = pl.BlockSpec((rows, ff_tile), lambda j: (0, j))
    return pl.pallas_call(
        split_tiles_kernel,
        grid=(wide // (2 * ff_tile),),
        in_specs=[pl.BlockSpec((rows, 2 * ff_tile), lambda j: (0, j))],
        out_specs=[out, out],
        out_shape=[jax.ShapeDtypeStruct((rows, wide // 2), f32)] * 2,
        compiler_params=params(),
        cost_estimate=cost(0, rows * wide * 6),
        name="split_tiles",
    )(both)


def norm_back_kernel(*refs, halves, extra):
    addends, refs = refs[: 2 * halves], refs[2 * halves :]
    grad = jnp.concatenate(
        [addends[2 * half][...].astype(f32) + addends[2 * half + 1][...].astype(f32) for half in range(halves)],
        axis=1,
    )
    if extra:
        grad, refs = grad + refs[0][...].astype(f32), refs[1:]
    base_ref, values_ref, scale_ref, gain_ref, out_ref, gain_grad_ref = refs
    scale = scale_ref[...]
    normed = values_ref[...].astype(f32) * scale
    weighted = grad * gain_ref[...]
    mean = jnp.mean(weighted * normed, axis=-1, keepdims=True)

    @pl.when(pl.program_id(0) == 0)
    def _():
        gain_grad_ref[...] = jnp.zeros_like(gain_grad_ref)

    gain_grad_ref[...] += jnp.sum(grad * normed, axis=0, keepdims=True)
    out_ref[...] = (base_ref[...].astype(f32) + scale * (weighted - normed * mean)).astype(bf16)


def norm_backward(addends, extra, base, values, scale, gain, tile=128):
    rows, width = base.shape
    row_spec = pl.BlockSpec((tile, width), lambda i: (i, 0))
    one_spec = pl.BlockSpec((1, width), lambda i: (0, 0))
    half_spec = pl.BlockSpec((tile, addends[0].shape[1]), lambda i: (i, 0))
    operands = list(addends) + ([extra] if extra is not None else []) + [base, values, scale, gain[None]]
    in_specs = [half_spec] * len(addends) + [row_spec] * (3 if extra is not None else 2)
    in_specs += [pl.BlockSpec((tile, 1), lambda i: (i, 0)), one_spec]
    return pl.pallas_call(
        partial(norm_back_kernel, halves=len(addends) // 2, extra=extra is not None),
        grid=(rows // tile,),
        in_specs=in_specs,
        out_specs=[row_spec, one_spec],
        out_shape=[jax.ShapeDtypeStruct((rows, width), bf16), jax.ShapeDtypeStruct((1, width), f32)],
        compiler_params=params(),
        cost_estimate=cost(rows * width * 20, rows * width * 12),
        name="norm_backward",
    )(*operands)


def ff_back_kernel(grad_ref, weight_ref, gate_factor_ref, up_factor_ref, out_ref):
    grad_hidden = dot_nn(grad_ref[...], weight_ref[...])
    out_ref[:, :ff_tile] = (grad_hidden * gate_factor_ref[...].astype(f32)).astype(bf16)
    out_ref[:, ff_tile:] = (grad_hidden * up_factor_ref[...].astype(f32)).astype(bf16)


def ff_backward(grad_out, weights, gate_factor, up_factor):
    count, depth = grad_out.shape
    units = gate_factor.shape[1]
    tiles = units // ff_tile
    factor = pl.BlockSpec((count, ff_tile), lambda j: (0, j))
    return pl.pallas_call(
        ff_back_kernel,
        grid=(tiles,),
        in_specs=[
            pl.BlockSpec((count, depth), lambda j: (0, 0)),
            pl.BlockSpec((depth, ff_tile), lambda j: (0, j + 2 * tiles)),
            factor,
            factor,
        ],
        out_specs=pl.BlockSpec((count, 2 * ff_tile), lambda j: (0, j)),
        out_shape=jax.ShapeDtypeStruct((count, 2 * units), bf16),
        compiler_params=params(),
        cost_estimate=cost(2 * count * depth * units, 2 * depth * units),
        name="ff_backward",
    )(grad_out, weights, gate_factor, up_factor)


def weight_grad_kernel(index_ref, left_own_ref, left_other_ref, own_ref, other_ref, *rest, pieces, block):
    out_ref, left_t = rest[-2:]
    rows = own_ref.shape[0]

    @pl.when(pl.program_id(0) == 0)
    def _():
        left_t[:, :rows] = left_own_ref[...].T
        left_t[:, rows:] = left_other_ref[...].T

    left = jnp.concatenate(
        [left_t[pl.ds(pl.multiple_of(index_ref[piece] * block, block), block)] for piece in range(pieces)],
        axis=0,
    )
    right = jnp.concatenate([own_ref[...], other_ref[...]], axis=0)
    product = dot_nn(left, right)
    for piece in range(pieces):
        part = product[piece * block : (piece + 1) * block]
        if len(rest) == 3:
            part = part + rest[0][piece].astype(f32)
        out_ref[piece] = part.astype(bf16)


def weight_grad(indices, rank, block, left, left_other, own, other, received=None):
    pieces = indices.shape[0]
    rows, wide = own.shape
    half = left.shape[1] // 2
    tile = next(size for size in (640, 512, 384, lanes) if wide % size == 0)
    out = pl.BlockSpec((pieces, block, tile), lambda j, s: (0, 0, j))
    left_spec = pl.BlockSpec((rows, half), lambda j, s: (0, s[pieces]))
    in_specs = [left_spec] * 2 + [pl.BlockSpec((rows, tile), lambda j, s: (0, j))] * 2
    operands = [left, left_other, own, other]
    if received is not None:
        in_specs.append(out)
        operands.append(received)
    return pl.pallas_call(
        partial(weight_grad_kernel, pieces=pieces, block=block),
        grid_spec=pltpu.PrefetchScalarGridSpec(
            num_scalar_prefetch=1,
            grid=(wide // tile,),
            in_specs=in_specs,
            out_specs=out,
            scratch_shapes=[pltpu.VMEM((half, 2 * rows), bf16)],
        ),
        out_shape=jax.ShapeDtypeStruct((pieces, block, wide), bf16),
        compiler_params=params(),
        cost_estimate=cost(4 * pieces * block * rows * wide, 2 * (pieces * block + 2 * rows) * wide),
        name="weight_grad",
    )(jnp.concatenate([indices, rank[None]]), *operands)


def gather_blocks_kernel(place_ref, *refs):
    count = (len(refs) - 2) // 1
    out_ref, sems = refs[-2:]
    copies = [
        pltpu.make_async_copy(refs[i], out_ref.at[place_ref[i]], sems.at[i]) for i in range(count)
    ]
    for copy in copies:
        copy.start()
    for copy in copies:
        copy.wait()


def gather_blocks(places, blocks):
    count = len(blocks)
    any_spec = pl.BlockSpec(memory_space=pl.ANY)
    return pl.pallas_call(
        gather_blocks_kernel,
        grid_spec=pltpu.PrefetchScalarGridSpec(
            num_scalar_prefetch=1,
            grid=(1,),
            in_specs=[any_spec] * count,
            out_specs=any_spec,
            scratch_shapes=[pltpu.SemaphoreType.DMA((count,))],
        ),
        out_shape=jax.ShapeDtypeStruct((count,) + blocks[0].shape, blocks[0].dtype),
        cost_estimate=cost(0, 2 * count * blocks[0].size * 2),
        name="gather_blocks",
    )(places, *blocks)


def after(values):
    return lax.optimization_barrier(values)


def on_device(
    prompt_states,
    continuation_states,
    continuation_offset,
    attention_gain,
    query_weight,
    key_weight,
    value_weight,
    query_gain,
    key_gain,
    output_weight,
    feedforward_gain,
    gate_weight,
    up_weight,
    down_weight,
    grad_prompt,
    grad_continuation,
):
    ring = lax.axis_size("ctx")
    tensor_size = lax.axis_size("tp")
    zsize, ysize = ring // 2, 2
    prompt_here, width = prompt_states.shape
    cont_length = continuation_states.shape[0]
    rows_here = prompt_here + cont_length
    prompt_length = prompt_here * ring
    head_size = query_gain.shape[0]
    query_width = query_weight.shape[1]
    local_heads = query_width // head_size
    shared_heads = key_weight.shape[1] // head_size
    group_size = local_heads * tensor_size // shared_heads
    pairs = local_heads // 2
    units = gate_weight.shape[1]
    half_width = width // 2
    block = half_width // ring
    low_head = [t * local_heads // group_size for t in range(tensor_size)]
    slot_count = max(
        ((t + 1) * local_heads - 1) // group_size - low_head[t] + 1 for t in range(tensor_size)
    )

    data_rank = lax.axis_index("dp")
    context_rank = lax.axis_index("ctx")
    tensor_rank = lax.axis_index("tp")
    zrank, yrank = context_rank // ysize, context_rank % ysize
    first_shared = tensor_rank * local_heads // group_size

    def z_pass(values, shift):
        pairs_of = [
            (z * ysize + y, (z + shift) % zsize * ysize + y) for z in range(zsize) for y in range(ysize)
        ]
        return lax.ppermute(values, "ctx", pairs_of)

    def y_swap(values):
        return lax.ppermute(values, "ctx", [(i, i ^ 1) for i in range(ring)])

    def dp_swap(values):
        return lax.ppermute(values, "dp", [(0, 1), (1, 0)])

    def tp_swap(values):
        return lax.ppermute(values, "tp", [(0, 1), (1, 0)])

    def shared_slots(weight):
        return lax.dynamic_slice_in_dim(weight, first_shared * head_size, slot_count * head_size, 1).reshape(
            -1, slot_count, head_size
        )

    def interleaved(gate, up):
        tiles = units // ff_tile
        both = jnp.stack([gate.reshape(-1, tiles, ff_tile), up.reshape(-1, tiles, ff_tile)], axis=2)
        return both.reshape(-1, 2 * units)

    key_value_weight = jnp.concatenate(
        [shared_slots(key_weight), shared_slots(value_weight)], axis=2
    ).reshape(-1, slot_count * lanes)
    qkv_width = query_width + slot_count * lanes
    attn_weights = lax.all_gather(
        jnp.concatenate([query_weight, key_value_weight, output_weight.T], axis=1),
        ("dp", "ctx"),
        axis=0,
        tiled=True,
    )
    ff_weights = lax.all_gather(
        jnp.concatenate([interleaved(gate_weight, up_weight), down_weight.T], axis=1),
        ("dp", "ctx"),
        axis=0,
        tiled=True,
    )
    qkv_weights = attn_weights[:, :qkv_width]
    shared_weights = attn_weights[:, query_width:qkv_width]
    out_weights_t = attn_weights[:, qkv_width:]

    row_ids = jnp.arange(rows_here, dtype=jnp.int32)
    positions = jnp.where(
        row_ids < prompt_here,
        context_rank * prompt_here + row_ids,
        prompt_length + continuation_offset[0] + row_ids - prompt_here,
    ).astype(f32)
    freqs = 10000.0 ** (-(2.0 * jnp.arange(head_size // 2, dtype=f32)) / head_size)
    angles = positions[:, None] * freqs[None, :]
    cosine, sine = jnp.cos(angles), jnp.sin(angles)
    cos_table = jnp.concatenate([cosine] * 4, axis=1)
    sin_table = jnp.concatenate([-sine, sine] * 2, axis=1)
    query_gain32, key_gain32 = query_gain.astype(f32), key_gain.astype(f32)
    gains = jnp.concatenate(
        [
            jnp.broadcast_to(jnp.concatenate([query_gain32] * 2), (pairs, 1, lanes)),
            jnp.broadcast_to(
                jnp.concatenate([key_gain32, jnp.ones((head_size,), f32)]), (slot_count, 1, lanes)
            ),
        ],
        axis=0,
    )
    steps = jnp.arange(zsize, dtype=jnp.int32)
    zs = (zrank + steps) % zsize
    own_blocks = zs * ysize + yrank
    other_blocks = zs * ysize + (1 - yrank)
    chunk_order = jnp.concatenate([own_blocks, other_blocks])
    key_places = jnp.repeat(chunk_order * prompt_here, prompt_here) + jnp.tile(
        jnp.arange(prompt_here, dtype=jnp.int32), ring
    )
    query_places = context_rank * prompt_here + jnp.arange(prompt_here, dtype=jnp.int32)
    prompt_mask = (key_places[None, :] <= query_places[:, None]).astype(f32)
    prompt_mask_t = (key_places[:, None] <= query_places[None, :]).astype(f32)
    slots = (
        (tensor_rank * local_heads + 2 * jnp.arange(pairs, dtype=jnp.int32)) // group_size - first_shared
    ).astype(jnp.int32)

    inputs_low = jnp.concatenate([prompt_states, continuation_states], axis=0)
    inputs = inputs_low.astype(f32)
    attn_gain32 = attention_gain.astype(f32)
    ff_gain32 = feedforward_gain.astype(f32)
    first_scale = lax.rsqrt(jnp.mean(inputs * inputs, axis=-1, keepdims=True) + epsilon)
    normed_low = (inputs * first_scale * attn_gain32).astype(bf16)
    raw = dot_nn(normed_low, qkv_weights)
    rotated = head_prep(raw, cos_table, sin_table, gains, pairs, head_size, 0.125)
    key_value = rotated[:, query_width:]
    own_chunk = key_value[:prompt_here]
    z_chunks = [own_chunk] + [z_pass(own_chunk, zsize - step) for step in range(1, zsize)]
    z_part = jnp.concatenate(z_chunks, axis=0)
    keys = jnp.concatenate([z_part, y_swap(z_part), key_value[prompt_here:]], axis=0)
    attended, inverse = attention_forward(
        slots, rotated, keys, prompt_mask, pairs, prompt_here, head_size
    )
    shared_weights = jnp.concatenate([shared_weights, tp_swap(shared_weights)], axis=1)
    attended, shared_weights = after((attended, shared_weights))
    attn_part = dot_nt(attended, out_weights_t).astype(bf16)
    resid32 = inputs + (attn_part.astype(f32) + tp_swap(attn_part).astype(f32))
    resid = resid32.astype(bf16)
    second_scale = lax.rsqrt(jnp.mean(resid32 * resid32, axis=-1, keepdims=True) + epsilon)
    normed_two = (resid32 * second_scale * ff_gain32).astype(bf16)
    hidden, gate_factor, up_factor = ff_forward(normed_two, ff_weights, units)

    def send_part(left, left_other, own, other):
        return weight_grad(other_blocks, data_rank, block, left, left_other, own, other)

    def keep_part(left, left_other, own, other, received):
        return weight_grad(own_blocks, data_rank, block, left, left_other, own, other, received)

    every_block = jnp.arange(ring, dtype=jnp.int32)

    def finish(kept):
        total = kept[0].astype(f32)
        for step in range(1, zsize):
            total = total + z_pass(kept[step], step).astype(f32)
        return total

    grad_out = jnp.concatenate([grad_prompt, grad_continuation], axis=0)
    out_pair = (grad_out, dp_swap(grad_out))
    two_pair = (normed_two, dp_swap(normed_two))
    one_pair = (normed_low, dp_swap(normed_low))
    hidden_other = dp_swap(hidden)

    grad_ff = ff_backward(grad_out, ff_weights, gate_factor, up_factor)
    grad_ff_other = dp_swap(grad_ff)
    down_grad = weight_grad(every_block, data_rank, block, *out_pair, hidden, hidden_other)
    grad_ff, down_grad = after((grad_ff, down_grad))
    down_done = lax.psum_scatter(down_grad, "ctx", scatter_dimension=0, tiled=True)[0]
    grad_parts = [matmul_nt(grad_ff, ff_weights, 0, 0, half_width)]
    grad_parts.append(matmul_nt(after((grad_ff, grad_parts[0]))[0], ff_weights, 0, half_width, half_width))
    grad_ff, hidden_next, second_part = after((grad_ff, hidden, grad_parts[1]))
    ff_grad = weight_grad(every_block, data_rank, block, *two_pair, grad_ff, grad_ff_other)
    ff_done = lax.psum_scatter(ff_grad, "ctx", scatter_dimension=0, tiled=True)[0]
    first_other, ff_grad, hidden_next = after((tp_swap(grad_parts[0]), ff_grad, hidden_next))
    ff_part = matmul_nt(hidden_next, ff_weights, 2)
    ff_part_other = tp_swap(ff_part)
    ff_part, second_other = after((ff_part, tp_swap(second_part)))
    grad_resid_low, grad_ff_gain = norm_backward(
        [grad_parts[0], first_other, second_part, second_other], None, grad_out, resid, second_scale, ff_gain32
    )
    resid_pair = (grad_resid_low, dp_swap(grad_resid_low))
    attended_other = dp_swap(attended)
    grad_attended = dot_nn(grad_resid_low, out_weights_t).astype(bf16)
    grad_query, grad_keys = attention_backward(
        slots,
        rotated,
        keys,
        prompt_mask_t,
        attended,
        inverse,
        grad_attended,
        pairs,
        slot_count,
        prompt_here,
        head_size,
    )
    grad_keys_prompt = grad_keys[:prompt_length].astype(bf16)
    half_prompt = prompt_length // 2
    grad_query_low, query_gain_parts = head_prep_back(
        raw, 0, grad_query, cos_table, sin_table, gains, False, head_size
    )
    query_parts = [
        dot_nt(grad_query_low, qkv_weights[half * half_width : (half + 1) * half_width, :query_width]).astype(bf16)
        for half in range(2)
    ]
    received_keys = y_swap(grad_keys_prompt[half_prompt:])
    received_keys, query_parts[0], query_parts[1] = after((received_keys, query_parts[0], query_parts[1]))
    query_others = [tp_swap(part) for part in query_parts]
    kept_keys = (grad_keys_prompt[:half_prompt].astype(f32) + received_keys.astype(f32)).astype(bf16)
    own_keys = kept_keys[:prompt_here].astype(f32)
    for step in range(1, zsize):
        own_keys = own_keys + z_pass(
            kept_keys[step * prompt_here : (step + 1) * prompt_here], step
        ).astype(f32)
    ff_part, ff_part_other, resid_out, kept_keys = after((ff_part, ff_part_other, resid, kept_keys))
    own_keys, query_others[0] = after((own_keys, query_others[0]))
    output = (resid_out.astype(f32) + (ff_part.astype(f32) + ff_part_other.astype(f32))).astype(bf16)
    grad_key_value = jnp.concatenate([own_keys, grad_keys[prompt_length:]], axis=0)
    out_sent = send_part(*resid_pair, attended, attended_other)
    grad_key_value, out_sent, output = after((grad_key_value, out_sent, output))
    grad_shared_low, key_gain_parts = head_prep_back(
        raw, pairs, grad_key_value, cos_table, sin_table, gains, True, head_size
    )
    grad_shared_other = tp_swap(grad_shared_low)
    grad_qkv = jnp.concatenate([grad_query_low, grad_shared_low], axis=1)
    grad_qkv_other = dp_swap(grad_qkv)
    qkv_sent = send_part(*one_pair, grad_qkv, grad_qkv_other)
    out_kept = keep_part(*resid_pair, attended, attended_other, y_swap(out_sent))
    qkv_kept = keep_part(*one_pair, grad_qkv, grad_qkv_other, y_swap(qkv_sent))
    grad_shared_other, query_others[1], out_kept, qkv_kept = after(
        (grad_shared_other, query_others[1], out_kept, qkv_kept)
    )
    shared_part = dot_nt(
        jnp.concatenate([grad_shared_low, grad_shared_other], axis=1), shared_weights
    ).astype(bf16)
    grad_input, grad_attn_gain = norm_backward(
        [query_parts[0], query_others[0], query_parts[1], query_others[1]],
        shared_part,
        grad_resid_low,
        inputs_low,
        first_scale,
        attn_gain32,
    )
    down_done = down_done.astype(f32).T
    gate_done, up_done = split_tiles(ff_done)
    out_done = finish(out_kept).T
    qkv_done = finish(qkv_kept)

    shared_done = qkv_done[:, query_width:]
    shared_other = tp_swap(shared_done)
    from_first = jnp.where(tensor_rank == 0, shared_done, shared_other)
    from_second = jnp.where(tensor_rank == 0, shared_other, shared_done)

    def all_heads(values, offset, which):
        block = values.reshape(-1, slot_count, 2, head_size)[:, :, which].reshape(-1, slot_count * head_size)
        before = offset * head_size
        after = shared_heads * head_size - before - slot_count * head_size
        return jnp.pad(block, ((0, 0), (before, after)))

    key_done, value_done = (
        all_heads(from_first, low_head[0], which) + all_heads(from_second, low_head[1], which)
        for which in range(2)
    )

    query_gain_sum = jnp.sum(query_gain_parts.reshape(-1, head_size), axis=0)
    key_gain_sum = jnp.sum(key_gain_parts[:, 0, :head_size], axis=0)
    gain_sums = jnp.concatenate([grad_attn_gain[0], grad_ff_gain[0], query_gain_sum, key_gain_sum]).reshape(-1, lanes)
    gain_sums = gain_sums + dp_swap(gain_sums)
    gain_sums = gain_sums + y_swap(gain_sums)
    gain_total = gain_sums
    for step in range(1, zsize):
        gain_total = gain_total + z_pass(gain_sums, step)
    gain_total = gain_total.reshape(-1)
    head_gains = gain_total[2 * width :]
    head_gains = head_gains + tp_swap(head_gains)
    return (
        output[:prompt_here],
        output[prompt_here:],
        grad_input[:prompt_here],
        grad_input[prompt_here:],
        gain_total[:width],
        qkv_done[:, :query_width],
        key_done,
        value_done,
        head_gains[:head_size],
        head_gains[head_size:],
        out_done,
        gain_total[width : 2 * width],
        gate_done,
        up_done,
        down_done,
    )


def solution(mesh):
    in_specs = (
        P(("dp", "ctx"), None),
        P(("dp", "ctx"), None),
        P(("dp", "ctx")),
        P(),
        P(("dp", "ctx"), "tp"),
        P(("dp", "ctx"), None),
        P(("dp", "ctx"), None),
        P(),
        P(),
        P("tp", ("dp", "ctx")),
        P(),
        P(("dp", "ctx"), "tp"),
        P(("dp", "ctx"), "tp"),
        P("tp", ("dp", "ctx")),
        P(("dp", "ctx"), None),
        P(("dp", "ctx"), None),
    )
    out_specs = (
        P(("dp", "ctx"), None),
        P(("dp", "ctx"), None),
        P(("dp", "ctx"), None),
        P(("dp", "ctx"), None),
        P(),
        P(("dp", "ctx"), "tp"),
        P(("dp", "ctx"), None),
        P(("dp", "ctx"), None),
        P(),
        P(),
        P("tp", ("dp", "ctx")),
        P(),
        P(("dp", "ctx"), "tp"),
        P(("dp", "ctx"), "tp"),
        P("tp", ("dp", "ctx")),
    )
    return jax.shard_map(
        on_device, mesh=mesh, in_specs=in_specs, out_specs=out_specs, check_vma=False
    )
```

```python
from functools import partial

import jax
import jax.numpy as jnp
from jax import lax
from jax.experimental import pallas as pl
from jax.experimental.pallas import tpu as pltpu
from jax.sharding import PartitionSpec as P

epsilon = 1e-06
bf16 = jnp.bfloat16
f32 = jnp.float32
lanes = 128


def params(megabytes=48):
    return pltpu.CompilerParams(vmem_limit_bytes=megabytes << 20)


def cost(flops, bytes_accessed, transcendentals=0, weight=1):
    return pl.CostEstimate(
        flops=int(flops * weight * 0.25),
        bytes_accessed=int(bytes_accessed * weight * 0.25),
        transcendentals=int(transcendentals * weight * 0.25),
    )


def dot_nn(left, right):
    return jnp.dot(left, right, preferred_element_type=f32)


def dot_nt(left, right):
    return lax.dot_general(left, right, (((1,), (1,)), ((), ())), preferred_element_type=f32)


def dot_tn(left, right):
    return lax.dot_general(left, right, (((0,), (0,)), ((), ())), preferred_element_type=f32)


def half_mask(shape, size):
    return lax.broadcasted_iota(jnp.int32, shape, 1) % (2 * size) < size


def swap_quarters(values, head_size):
    quarter = head_size // 2
    low = half_mask(values.shape, quarter)
    return jnp.where(low, pltpu.roll(values, lanes - quarter, 1), pltpu.roll(values, quarter, 1))


def head_sums(values, low):
    first = jnp.sum(jnp.where(low, values, 0.0), axis=1, keepdims=True)
    second = jnp.sum(jnp.where(low, 0.0, values), axis=1, keepdims=True)
    return jnp.where(low, first, second)


def prep_kernel(raw_ref, cos_ref, sin_ref, gain_ref, out_ref, *, query_blocks, head_size, scale):
    block = pl.program_id(0)
    raw = raw_ref[...]
    low = half_mask(raw.shape, head_size)
    inverse = lax.rsqrt(head_sums(raw * raw, low) * (1.0 / head_size) + epsilon)
    normed = raw * inverse * gain_ref[0]
    rotated = normed * cos_ref[...] + swap_quarters(normed, head_size) * sin_ref[...]
    is_query = block < query_blocks
    rotated = rotated * jnp.where(is_query, scale, 1.0)
    out_ref[...] = jnp.where(jnp.logical_or(is_query, low), rotated, raw).astype(bf16)


def head_prep(raw, cos_table, sin_table, gains, query_blocks, head_size, scale):
    rows, width = raw.shape
    return pl.pallas_call(
        partial(prep_kernel, query_blocks=query_blocks, head_size=head_size, scale=scale),
        grid=(width // lanes,),
        in_specs=[
            pl.BlockSpec((rows, lanes), lambda i: (0, i)),
            pl.BlockSpec((rows, lanes), lambda i: (0, 0)),
            pl.BlockSpec((rows, lanes), lambda i: (0, 0)),
            pl.BlockSpec((1, 1, lanes), lambda i: (i, 0, 0)),
        ],
        out_specs=pl.BlockSpec((rows, lanes), lambda i: (0, i)),
        out_shape=jax.ShapeDtypeStruct((rows, width), bf16),
        compiler_params=params(),
        cost_estimate=cost(rows * width * 40, rows * width * 6),
        name="head_prep",
    )(raw, cos_table, sin_table, gains)


def prep_back_kernel(
    raw_ref, grad_ref, cos_ref, sin_ref, gain_ref, out_ref, gain_out_ref, *, has_value, head_size
):
    raw = raw_ref[...]
    grad = grad_ref[...]
    low = half_mask(raw.shape, head_size)
    turned = grad * cos_ref[...] + swap_quarters(grad * sin_ref[...], head_size)
    inverse = lax.rsqrt(head_sums(raw * raw, low) * (1.0 / head_size) + epsilon)
    normed = raw * inverse
    weighted = turned * gain_ref[0]
    mean = head_sums(weighted * normed, low) * (1.0 / head_size)
    result = inverse * (weighted - normed * mean)
    if has_value:
        result = jnp.where(low, result, grad)
    out_ref[...] = result.astype(bf16)
    gain_out_ref[0] = jnp.sum(turned * normed, axis=0, keepdims=True)


def head_prep_back(raw, raw_block, grad, cos_table, sin_table, gains, has_value, head_size):
    rows, width = grad.shape
    blocks = width // lanes
    return pl.pallas_call(
        partial(prep_back_kernel, has_value=has_value, head_size=head_size),
        grid=(blocks,),
        in_specs=[
            pl.BlockSpec((rows, lanes), lambda i: (0, i + raw_block)),
            pl.BlockSpec((rows, lanes), lambda i: (0, i)),
            pl.BlockSpec((rows, lanes), lambda i: (0, 0)),
            pl.BlockSpec((rows, lanes), lambda i: (0, 0)),
            pl.BlockSpec((1, 1, lanes), lambda i: (i + raw_block, 0, 0)),
        ],
        out_specs=[
            pl.BlockSpec((rows, lanes), lambda i: (0, i)),
            pl.BlockSpec((1, 1, lanes), lambda i: (i, 0, 0)),
        ],
        out_shape=[
            jax.ShapeDtypeStruct((rows, width), bf16),
            jax.ShapeDtypeStruct((blocks, 1, lanes), f32),
        ],
        compiler_params=params(),
        cost_estimate=cost(rows * width * 60, rows * width * 10),
        name="head_prep_back",
    )(raw, grad, cos_table, sin_table, gains)


def head_lanes(pair, index, head_size):
    values = pair.astype(f32)
    if index:
        values = pltpu.roll(values, head_size, 1)
    return jnp.where(half_mask(values.shape, head_size), values, 0.0)


def diagonal_mask(keys, rows):
    return lax.broadcasted_iota(jnp.int32, (keys, rows), 0) <= lax.broadcasted_iota(
        jnp.int32, (keys, rows), 1
    )


def attn_fwd_kernel(
    slot_ref, query_ref, keys_ref, mask_ref, out_ref, inverse_ref, acc, *, prompt_here, chunk, head_size
):
    rows = query_ref.shape[0]
    prompt_keys = mask_ref.shape[1]
    cont = rows - prompt_here
    half = cont // 2
    pair = query_ref[...]
    low = half_mask((1, lanes), head_size)
    results = []
    for index in range(2):
        query = head_lanes(pair, index, head_size).astype(bf16)

        def weigh(scores, keyvalue):
            ones_value = jnp.where(low, jnp.ones((), bf16), keyvalue)
            return dot_nn(jnp.exp(scores).astype(bf16), ones_value)

        keyvalue = keys_ref[0:prompt_keys]
        scores = dot_nt(query[:prompt_here], keyvalue)
        weights = (jnp.exp(scores) * mask_ref[...]).astype(bf16)
        acc[0:prompt_here] = dot_nn(weights, jnp.where(low, jnp.ones((), bf16), keyvalue))

        acc[prompt_here:rows] = jnp.zeros((cont, lanes), f32)
        cont_query = query[prompt_here:]

        def prompt_step(step, carry):
            piece = keys_ref[pl.ds(pl.multiple_of(step * chunk, chunk), chunk)]
            acc[prompt_here:rows] += weigh(dot_nt(cont_query, piece), piece)
            return carry

        lax.fori_loop(0, prompt_keys // chunk, prompt_step, 0)
        for block in range(2):
            start = prompt_here + block * half
            piece = keys_ref[prompt_keys + block * half : prompt_keys + (block + 1) * half]
            scores = dot_nt(query[start:], piece)
            row_ids = lax.broadcasted_iota(jnp.int32, scores.shape, 0)
            key_ids = lax.broadcasted_iota(jnp.int32, scores.shape, 1)
            acc[start:rows] += weigh(jnp.where(key_ids <= row_ids, scores, -1e30), piece)
        total = acc[...]
        results.append((total, pltpu.roll(total, head_size, 1)))
    first, first_moved = results[0]
    second, second_moved = results[1]
    full_low = half_mask((rows, lanes), head_size)
    inverse = 1.0 / jnp.where(full_low, first, second_moved)
    inverse_ref[...] = inverse
    out_ref[...] = (jnp.where(full_low, first_moved, second) * inverse).astype(bf16)


def attention_forward(slots, rotated, keys, prompt_mask, pairs, prompt_here, head_size):
    rows = rotated.shape[0]
    key_count = keys.shape[0]
    prompt_keys = prompt_mask.shape[1]
    chunk = min(512, prompt_keys)
    elements = 2 * pairs * rows * key_count
    return pl.pallas_call(
        partial(attn_fwd_kernel, prompt_here=prompt_here, chunk=chunk, head_size=head_size),
        grid_spec=pltpu.PrefetchScalarGridSpec(
            num_scalar_prefetch=1,
            grid=(pairs,),
            in_specs=[
                pl.BlockSpec((rows, lanes), lambda p, s: (0, p)),
                pl.BlockSpec((key_count, lanes), lambda p, s: (0, s[p])),
                pl.BlockSpec(prompt_mask.shape, lambda p, s: (0, 0)),
            ],
            out_specs=[
                pl.BlockSpec((rows, lanes), lambda p, s: (0, p)),
                pl.BlockSpec((rows, lanes), lambda p, s: (0, p)),
            ],
            scratch_shapes=[pltpu.VMEM((rows, lanes), f32)],
        ),
        out_shape=[
            jax.ShapeDtypeStruct((rows, pairs * lanes), bf16),
            jax.ShapeDtypeStruct((rows, pairs * lanes), f32),
        ],
        compiler_params=params(),
        cost_estimate=cost(elements * 1000, elements, elements),
        name="attention_forward",
    )(slots, rotated, keys, prompt_mask)


def attn_back_kernel(
    slot_ref,
    query_ref,
    keys_ref,
    mask_ref,
    attended_ref,
    inverse_ref,
    grad_ref,
    grad_query_ref,
    grad_keys_ref,
    q_sc,
    g_sc,
    d_sc,
    dq_sc,
    *,
    prompt_here,
    chunk,
    head_size,
):
    step_id = pl.program_id(0)
    rows = query_ref.shape[0]
    prompt_keys = mask_ref.shape[0]
    cont = rows - prompt_here
    half = cont // 2
    low = half_mask((1, lanes), head_size)
    full_low = half_mask((rows, lanes), head_size)
    lane_ids = lax.broadcasted_iota(jnp.int32, (rows, lanes), 1)

    fresh = jnp.logical_or(
        step_id == 0, slot_ref[step_id] != slot_ref[jnp.maximum(step_id - 1, 0)]
    )

    @pl.when(fresh)
    def _():
        grad_keys_ref[...] = jnp.zeros_like(grad_keys_ref)

    pair = query_ref[...]
    grad_pair = grad_ref[...].astype(f32)
    inverse = inverse_ref[...]
    product = grad_pair * attended_ref[...].astype(f32)
    delta = head_sums(product, full_low) * inverse
    scaled = grad_pair * inverse
    for index in range(2):
        grad_high = scaled if index else pltpu.roll(scaled, head_size, 1)
        delta_low = pltpu.roll(delta, head_size, 1) if index else delta
        delta_high_part = delta_low.astype(bf16).astype(f32)
        extra = jnp.where(
            lane_ids == 0, -delta_high_part, jnp.where(lane_ids == 1, delta_high_part - delta_low, 0.0)
        )
        q_sc[index] = head_lanes(pair, index, head_size).astype(bf16)
        g_sc[index] = jnp.where(full_low, 0.0, grad_high).astype(bf16)
        d_sc[index] = jnp.where(full_low, extra, grad_high).astype(bf16)
    dq_sc[...] = jnp.zeros_like(dq_sc)

    def block(key_start, key_size, row_start, row_stop, mask):
        piece = keys_ref[pl.ds(key_start, key_size)]
        ones_value = jnp.where(low, jnp.ones((), bf16), piece)
        count = row_stop - row_start

        def rows_of(ref):
            return jnp.concatenate([ref[0, row_start:row_stop], ref[1, row_start:row_stop]], axis=0)

        query = rows_of(q_sc)
        weights = jnp.exp(dot_nt(piece, query))
        if mask is not None:
            weights = mask(weights)
        grad_scores = (weights * dot_nt(ones_value, rows_of(d_sc))).astype(bf16)
        grad_keys_ref[pl.ds(key_start, key_size)] += dot_nn(grad_scores, query) + dot_nn(
            weights.astype(bf16), rows_of(g_sc)
        )
        grad_query = dot_tn(grad_scores, piece)
        dq_sc[0, row_start:row_stop] += grad_query[:count]
        dq_sc[1, row_start:row_stop] += grad_query[count:]

    def prompt_mask(weights):
        mask = mask_ref[...]
        return weights * jnp.concatenate([mask, mask], axis=1)

    block(0, prompt_keys, 0, prompt_here, prompt_mask)

    def prompt_step(step, carry):
        block(pl.multiple_of(step * chunk, chunk), chunk, prompt_here, rows, None)
        return carry

    lax.fori_loop(0, prompt_keys // chunk, prompt_step, 0)
    for part in range(2):
        start = prompt_here + part * half

        def causal(weights, size=rows - start):
            key_ids = lax.broadcasted_iota(jnp.int32, weights.shape, 0)
            row_ids = lax.broadcasted_iota(jnp.int32, weights.shape, 1)
            row_ids = jnp.where(row_ids < size, row_ids, row_ids - size)
            return jnp.where(key_ids <= row_ids, weights, 0.0)

        block(prompt_keys + part * half, half, start, rows, causal)
    moved = pltpu.roll(dq_sc[1], head_size, 1)
    grad_query_ref[...] = jnp.where(full_low, dq_sc[0], moved) * 0.125


def attention_backward(
    slots, rotated, keys, prompt_mask_t, attended, inverse, grad_attended, pairs, slot_count, prompt_here, head_size
):
    rows = rotated.shape[0]
    key_count = keys.shape[0]
    prompt_keys = prompt_mask_t.shape[0]
    chunk = min(512, prompt_keys)
    elements = 2 * pairs * rows * key_count
    pair_spec = pl.BlockSpec((rows, lanes), lambda p, s: (0, p))
    return pl.pallas_call(
        partial(attn_back_kernel, prompt_here=prompt_here, chunk=chunk, head_size=head_size),
        grid_spec=pltpu.PrefetchScalarGridSpec(
            num_scalar_prefetch=1,
            grid=(pairs,),
            in_specs=[
                pair_spec,
                pl.BlockSpec((key_count, lanes), lambda p, s: (0, s[p])),
                pl.BlockSpec(prompt_mask_t.shape, lambda p, s: (0, 0)),
                pair_spec,
                pair_spec,
                pair_spec,
            ],
            out_specs=[
                pair_spec,
                pl.BlockSpec((key_count, lanes), lambda p, s: (0, s[p])),
            ],
            scratch_shapes=[
                pltpu.VMEM((2, rows, lanes), bf16),
                pltpu.VMEM((2, rows, lanes), bf16),
                pltpu.VMEM((2, rows, lanes), bf16),
                pltpu.VMEM((2, rows, lanes), f32),
            ],
        ),
        out_shape=[
            jax.ShapeDtypeStruct((rows, pairs * lanes), f32),
            jax.ShapeDtypeStruct((key_count, slot_count * lanes), f32),
        ],
        compiler_params=params(),
        cost_estimate=cost(elements * 2500, elements, elements, 1),
        name="attention_backward",
    )(slots, rotated, keys, prompt_mask_t, attended, inverse, grad_attended)


ff_tile = 256


def ff_forward_kernel(rows_ref, weight_ref, hidden_ref, gate_factor_ref, up_factor_ref):
    both = dot_nn(rows_ref[...], weight_ref[...])
    gate, up = both[:, :ff_tile], both[:, ff_tile:]
    sigmoid = 1.0 / (1.0 + jnp.exp(-gate))
    silu = gate * sigmoid
    hidden_ref[...] = (silu * up).astype(bf16)
    gate_factor_ref[...] = (up * sigmoid * (1.0 + gate * (1.0 - sigmoid))).astype(bf16)
    up_factor_ref[...] = silu.astype(bf16)


def ff_forward(rows, weights, units):
    count, depth = rows.shape
    out = pl.BlockSpec((count, ff_tile), lambda j: (0, j))
    return pl.pallas_call(
        ff_forward_kernel,
        grid=(units // ff_tile,),
        in_specs=[
            pl.BlockSpec((count, depth), lambda j: (0, 0)),
            pl.BlockSpec((depth, 2 * ff_tile), lambda j: (0, j)),
        ],
        out_specs=[out, out, out],
        out_shape=[jax.ShapeDtypeStruct((count, units), bf16)] * 3,
        compiler_params=params(),
        cost_estimate=cost(4 * count * depth * units, 4 * depth * units, count * units),
        name="ff_forward",
    )(rows, weights)


def matmul_nt_kernel(left_ref, right_ref, out_ref):
    out_ref[...] = dot_nt(left_ref[...], right_ref[...]).astype(bf16)


def matmul_nt(left, weights, column_block, first=0, wide=None, tile=256):
    count, depth = left.shape
    wide = wide or weights.shape[0]
    return pl.pallas_call(
        matmul_nt_kernel,
        grid=(wide // tile,),
        in_specs=[
            pl.BlockSpec((count, depth), lambda j: (0, 0)),
            pl.BlockSpec((tile, depth), lambda j: (j + first // tile, column_block)),
        ],
        out_specs=pl.BlockSpec((count, tile), lambda j: (0, j)),
        out_shape=jax.ShapeDtypeStruct((count, wide), bf16),
        compiler_params=params(),
        cost_estimate=cost(2 * count * depth * wide, 2 * depth * wide),
        name="matmul_nt",
    )(left, weights)


def split_tiles_kernel(*refs, bounds):
    gate_ref, up_ref = refs[-2:]
    step = pl.program_id(0)
    for part_ref, start, stop in zip(refs, bounds, bounds[1:]):

        @pl.when(jnp.logical_and(step >= start, step < stop))
        def _(part_ref=part_ref):
            gate_ref[...] = part_ref[:, :ff_tile].astype(f32)
            up_ref[...] = part_ref[:, ff_tile:].astype(f32)


def split_tiles(parts):
    rows = parts[0].shape[0]
    bounds = [0]
    for part in parts:
        bounds.append(bounds[-1] + part.shape[1] // (2 * ff_tile))
    out = pl.BlockSpec((rows, ff_tile), lambda j: (0, j))
    in_specs = [
        pl.BlockSpec(
            (rows, 2 * ff_tile),
            lambda j, start=start, stop=stop: (0, jnp.clip(j - start, 0, stop - start - 1)),
        )
        for start, stop in zip(bounds, bounds[1:])
    ]
    return pl.pallas_call(
        partial(split_tiles_kernel, bounds=bounds),
        grid=(bounds[-1],),
        in_specs=in_specs,
        out_specs=[out, out],
        out_shape=[jax.ShapeDtypeStruct((rows, bounds[-1] * ff_tile), f32)] * 2,
        compiler_params=params(),
        cost_estimate=cost(0, rows * bounds[-1] * ff_tile * 12),
        name="split_tiles",
    )(*parts)


def norm_back_kernel(*refs, halves, extra):
    addends, refs = refs[: 2 * halves], refs[2 * halves :]
    grad = jnp.concatenate(
        [addends[2 * half][...].astype(f32) + addends[2 * half + 1][...].astype(f32) for half in range(halves)],
        axis=1,
    )
    if extra:
        grad, refs = grad + refs[0][...].astype(f32), refs[1:]
    base_ref, values_ref, scale_ref, gain_ref, out_ref, gain_grad_ref = refs
    scale = scale_ref[...]
    normed = values_ref[...].astype(f32) * scale
    weighted = grad * gain_ref[...]
    mean = jnp.mean(weighted * normed, axis=-1, keepdims=True)

    @pl.when(pl.program_id(0) == 0)
    def _():
        gain_grad_ref[...] = jnp.zeros_like(gain_grad_ref)

    gain_grad_ref[...] += jnp.sum(grad * normed, axis=0, keepdims=True)
    out_ref[...] = (base_ref[...].astype(f32) + scale * (weighted - normed * mean)).astype(bf16)


def norm_backward(addends, extra, base, values, scale, gain, tile=128):
    rows, width = base.shape
    row_spec = pl.BlockSpec((tile, width), lambda i: (i, 0))
    one_spec = pl.BlockSpec((1, width), lambda i: (0, 0))
    half_spec = pl.BlockSpec((tile, addends[0].shape[1]), lambda i: (i, 0))
    operands = list(addends) + ([extra] if extra is not None else []) + [base, values, scale, gain[None]]
    in_specs = [half_spec] * len(addends) + [row_spec] * (3 if extra is not None else 2)
    in_specs += [pl.BlockSpec((tile, 1), lambda i: (i, 0)), one_spec]
    return pl.pallas_call(
        partial(norm_back_kernel, halves=len(addends) // 2, extra=extra is not None),
        grid=(rows // tile,),
        in_specs=in_specs,
        out_specs=[row_spec, one_spec],
        out_shape=[jax.ShapeDtypeStruct((rows, width), bf16), jax.ShapeDtypeStruct((1, width), f32)],
        compiler_params=params(),
        cost_estimate=cost(rows * width * 20, rows * width * 12),
        name="norm_backward",
    )(*operands)


def ff_back_kernel(grad_ref, weight_ref, gate_factor_ref, up_factor_ref, out_ref):
    grad_hidden = dot_nn(grad_ref[...], weight_ref[...])
    out_ref[:, :ff_tile] = (grad_hidden * gate_factor_ref[...].astype(f32)).astype(bf16)
    out_ref[:, ff_tile:] = (grad_hidden * up_factor_ref[...].astype(f32)).astype(bf16)


def ff_backward(grad_out, weights, gate_factor, up_factor):
    count, depth = grad_out.shape
    units = gate_factor.shape[1]
    tiles = units // ff_tile
    factor = pl.BlockSpec((count, ff_tile), lambda j: (0, j))
    return pl.pallas_call(
        ff_back_kernel,
        grid=(tiles,),
        in_specs=[
            pl.BlockSpec((count, depth), lambda j: (0, 0)),
            pl.BlockSpec((depth, ff_tile), lambda j: (0, j + 2 * tiles)),
            factor,
            factor,
        ],
        out_specs=pl.BlockSpec((count, 2 * ff_tile), lambda j: (0, j)),
        out_shape=jax.ShapeDtypeStruct((count, 2 * units), bf16),
        compiler_params=params(),
        cost_estimate=cost(2 * count * depth * units, 2 * depth * units),
        name="ff_backward",
    )(grad_out, weights, gate_factor, up_factor)


def weight_grad_kernel(index_ref, left_own_ref, left_other_ref, own_ref, other_ref, *rest, pieces, block):
    out_ref, left_t = rest[-2:]
    rows = own_ref.shape[0]

    @pl.when(pl.program_id(0) == 0)
    def _():
        left_t[:, :rows] = left_own_ref[...].T
        left_t[:, rows:] = left_other_ref[...].T

    left = jnp.concatenate(
        [left_t[pl.ds(pl.multiple_of(index_ref[piece] * block, block), block)] for piece in range(pieces)],
        axis=0,
    )
    right = jnp.concatenate([own_ref[...], other_ref[...]], axis=0)
    product = dot_nn(left, right)
    for piece in range(pieces):
        part = product[piece * block : (piece + 1) * block]
        if len(rest) == 3:
            part = part + rest[0][piece].astype(f32)
        out_ref[piece] = part.astype(bf16)


def weight_grad(indices, rank, block, left, left_other, own, other, received=None, first=0, wide=None):
    pieces = indices.shape[0]
    rows = own.shape[0]
    wide = wide or own.shape[1]
    half = left.shape[1] // 2
    tile = next(size for size in (640, 512, 384, lanes) if wide % size == 0 and first % size == 0)
    out = pl.BlockSpec((pieces, block, tile), lambda j, s: (0, 0, j))
    left_spec = pl.BlockSpec((rows, half), lambda j, s: (0, s[pieces]))
    in_specs = [left_spec] * 2 + [pl.BlockSpec((rows, tile), lambda j, s: (0, j + first // tile))] * 2
    operands = [left, left_other, own, other]
    if received is not None:
        in_specs.append(pl.BlockSpec((pieces, block, tile), lambda j, s: (0, 0, j)))
        operands.append(received)
    return pl.pallas_call(
        partial(weight_grad_kernel, pieces=pieces, block=block),
        grid_spec=pltpu.PrefetchScalarGridSpec(
            num_scalar_prefetch=1,
            grid=(wide // tile,),
            in_specs=in_specs,
            out_specs=out,
            scratch_shapes=[pltpu.VMEM((half, 2 * rows), bf16)],
        ),
        out_shape=jax.ShapeDtypeStruct((pieces, block, wide), bf16),
        compiler_params=params(),
        cost_estimate=cost(4 * pieces * block * rows * wide, 2 * (pieces * block + 2 * rows) * wide),
        name="weight_grad",
    )(jnp.concatenate([indices, rank[None]]), *operands)


def gather_blocks_kernel(place_ref, *refs):
    count = (len(refs) - 2) // 1
    out_ref, sems = refs[-2:]
    copies = [
        pltpu.make_async_copy(refs[i], out_ref.at[place_ref[i]], sems.at[i]) for i in range(count)
    ]
    for copy in copies:
        copy.start()
    for copy in copies:
        copy.wait()


def gather_blocks(places, blocks):
    count = len(blocks)
    any_spec = pl.BlockSpec(memory_space=pl.ANY)
    return pl.pallas_call(
        gather_blocks_kernel,
        grid_spec=pltpu.PrefetchScalarGridSpec(
            num_scalar_prefetch=1,
            grid=(1,),
            in_specs=[any_spec] * count,
            out_specs=any_spec,
            scratch_shapes=[pltpu.SemaphoreType.DMA((count,))],
        ),
        out_shape=jax.ShapeDtypeStruct((count,) + blocks[0].shape, blocks[0].dtype),
        cost_estimate=cost(0, 2 * count * blocks[0].size * 2),
        name="gather_blocks",
    )(places, *blocks)


def after(values):
    return lax.optimization_barrier(values)


def on_device(
    prompt_states,
    continuation_states,
    continuation_offset,
    attention_gain,
    query_weight,
    key_weight,
    value_weight,
    query_gain,
    key_gain,
    output_weight,
    feedforward_gain,
    gate_weight,
    up_weight,
    down_weight,
    grad_prompt,
    grad_continuation,
):
    ring = lax.axis_size("ctx")
    tensor_size = lax.axis_size("tp")
    zsize, ysize = ring // 2, 2
    prompt_here, width = prompt_states.shape
    cont_length = continuation_states.shape[0]
    rows_here = prompt_here + cont_length
    prompt_length = prompt_here * ring
    head_size = query_gain.shape[0]
    query_width = query_weight.shape[1]
    local_heads = query_width // head_size
    shared_heads = key_weight.shape[1] // head_size
    group_size = local_heads * tensor_size // shared_heads
    pairs = local_heads // 2
    units = gate_weight.shape[1]
    half_width = width // 2
    block = half_width // ring
    low_head = [t * local_heads // group_size for t in range(tensor_size)]
    slot_count = max(
        ((t + 1) * local_heads - 1) // group_size - low_head[t] + 1 for t in range(tensor_size)
    )

    data_rank = lax.axis_index("dp")
    context_rank = lax.axis_index("ctx")
    tensor_rank = lax.axis_index("tp")
    zrank, yrank = context_rank // ysize, context_rank % ysize
    first_shared = tensor_rank * local_heads // group_size

    def z_pass(values, shift):
        pairs_of = [
            (z * ysize + y, (z + shift) % zsize * ysize + y) for z in range(zsize) for y in range(ysize)
        ]
        return lax.ppermute(values, "ctx", pairs_of)

    def y_swap(values):
        return lax.ppermute(values, "ctx", [(i, i ^ 1) for i in range(ring)])

    def dp_swap(values):
        return lax.ppermute(values, "dp", [(0, 1), (1, 0)])

    def tp_swap(values):
        return lax.ppermute(values, "tp", [(0, 1), (1, 0)])

    def shared_slots(weight):
        return lax.dynamic_slice_in_dim(weight, first_shared * head_size, slot_count * head_size, 1).reshape(
            -1, slot_count, head_size
        )

    def interleaved(gate, up):
        tiles = units // ff_tile
        both = jnp.stack([gate.reshape(-1, tiles, ff_tile), up.reshape(-1, tiles, ff_tile)], axis=2)
        return both.reshape(-1, 2 * units)

    key_value_weight = jnp.concatenate(
        [shared_slots(key_weight), shared_slots(value_weight)], axis=2
    ).reshape(-1, slot_count * lanes)
    qkv_width = query_width + slot_count * lanes
    attn_weights = lax.all_gather(
        jnp.concatenate([query_weight, key_value_weight, output_weight.T], axis=1),
        ("dp", "ctx"),
        axis=0,
        tiled=True,
    )
    ff_weights = lax.all_gather(
        jnp.concatenate([interleaved(gate_weight, up_weight), down_weight.T], axis=1),
        ("dp", "ctx"),
        axis=0,
        tiled=True,
    )
    qkv_weights = attn_weights[:, :qkv_width]
    shared_weights = attn_weights[:, query_width:qkv_width]
    out_weights_t = attn_weights[:, qkv_width:]

    row_ids = jnp.arange(rows_here, dtype=jnp.int32)
    positions = jnp.where(
        row_ids < prompt_here,
        context_rank * prompt_here + row_ids,
        prompt_length + continuation_offset[0] + row_ids - prompt_here,
    ).astype(f32)
    freqs = 10000.0 ** (-(2.0 * jnp.arange(head_size // 2, dtype=f32)) / head_size)
    angles = positions[:, None] * freqs[None, :]
    cosine, sine = jnp.cos(angles), jnp.sin(angles)
    cos_table = jnp.concatenate([cosine] * 4, axis=1)
    sin_table = jnp.concatenate([-sine, sine] * 2, axis=1)
    query_gain32, key_gain32 = query_gain.astype(f32), key_gain.astype(f32)
    gains = jnp.concatenate(
        [
            jnp.broadcast_to(jnp.concatenate([query_gain32] * 2), (pairs, 1, lanes)),
            jnp.broadcast_to(
                jnp.concatenate([key_gain32, jnp.ones((head_size,), f32)]), (slot_count, 1, lanes)
            ),
        ],
        axis=0,
    )
    steps = jnp.arange(zsize, dtype=jnp.int32)
    zs = (zrank + steps) % zsize
    own_blocks = zs * ysize + yrank
    other_blocks = zs * ysize + (1 - yrank)
    chunk_order = jnp.concatenate([own_blocks, other_blocks])
    key_places = jnp.repeat(chunk_order * prompt_here, prompt_here) + jnp.tile(
        jnp.arange(prompt_here, dtype=jnp.int32), ring
    )
    query_places = context_rank * prompt_here + jnp.arange(prompt_here, dtype=jnp.int32)
    prompt_mask = (key_places[None, :] <= query_places[:, None]).astype(f32)
    prompt_mask_t = (key_places[:, None] <= query_places[None, :]).astype(f32)
    slots = (
        (tensor_rank * local_heads + 2 * jnp.arange(pairs, dtype=jnp.int32)) // group_size - first_shared
    ).astype(jnp.int32)

    inputs_low = jnp.concatenate([prompt_states, continuation_states], axis=0)
    inputs = inputs_low.astype(f32)
    attn_gain32 = attention_gain.astype(f32)
    ff_gain32 = feedforward_gain.astype(f32)
    first_scale = lax.rsqrt(jnp.mean(inputs * inputs, axis=-1, keepdims=True) + epsilon)
    normed_low = (inputs * first_scale * attn_gain32).astype(bf16)
    raw = dot_nn(normed_low, qkv_weights)
    rotated = head_prep(raw, cos_table, sin_table, gains, pairs, head_size, 0.125)
    key_value = rotated[:, query_width:]
    own_chunk = key_value[:prompt_here]
    z_chunks = [own_chunk] + [z_pass(own_chunk, zsize - step) for step in range(1, zsize)]
    z_part = jnp.concatenate(z_chunks, axis=0)
    keys = jnp.concatenate([z_part, y_swap(z_part), key_value[prompt_here:]], axis=0)
    attended, inverse = attention_forward(
        slots, rotated, keys, prompt_mask, pairs, prompt_here, head_size
    )
    shared_weights = jnp.concatenate([shared_weights, tp_swap(shared_weights)], axis=1)
    attended, shared_weights = after((attended, shared_weights))
    attn_part = dot_nt(attended, out_weights_t).astype(bf16)
    resid32 = inputs + (attn_part.astype(f32) + tp_swap(attn_part).astype(f32))
    resid = resid32.astype(bf16)
    second_scale = lax.rsqrt(jnp.mean(resid32 * resid32, axis=-1, keepdims=True) + epsilon)
    normed_two = (resid32 * second_scale * ff_gain32).astype(bf16)
    grad_out = jnp.concatenate([grad_prompt, grad_continuation], axis=0)
    normed_two, two_other, out_other, one_other, attended_other = after(
        (normed_two, dp_swap(normed_two), dp_swap(grad_out), dp_swap(normed_low), dp_swap(attended))
    )
    hidden, gate_factor, up_factor = ff_forward(normed_two, ff_weights, units)

    def send_part(left, left_other, own, other, order=None, **span):
        indices = (steps if order is None else order) * ysize + 1 - yrank
        return weight_grad(indices, data_rank, block, left, left_other, own, other, **span)

    def keep_part(left, left_other, own, other, received, order=None, **span):
        indices = (steps if order is None else order) * ysize + yrank
        return weight_grad(indices, data_rank, block, left, left_other, own, other, received, **span)

    z_groups = [[z * ysize + y for z in range(zsize)] for y in range(ysize)]

    def z_scattered(kept):
        scattered = lax.psum_scatter(
            kept, "ctx", scatter_dimension=0, axis_index_groups=z_groups, tiled=True
        )
        return scattered[0]

    def finish(kept):
        total = kept[0].astype(f32)
        for step in range(1, zsize):
            total = total + z_pass(kept[step], step).astype(f32)
        return total

    out_pair, two_pair, one_pair = (grad_out, out_other), (normed_two, two_other), (normed_low, one_other)

    grad_ff = ff_backward(grad_out, ff_weights, gate_factor, up_factor)
    hidden_other, grad_ff = after((dp_swap(hidden), grad_ff))
    grad_ff_other = dp_swap(grad_ff)
    down_sent = send_part(*out_pair, hidden, hidden_other)
    hidden, grad_ff, down_sent = after((hidden, grad_ff, down_sent))
    first_part = matmul_nt(grad_ff, ff_weights, 0, 0, half_width)
    grad_ff, first_part = after((grad_ff, first_part))
    second_part = matmul_nt(grad_ff, ff_weights, 0, half_width, half_width)
    grad_ff, hidden_next, second_part = after((grad_ff, hidden, second_part))
    ff_pair = (grad_ff, grad_ff_other)
    ff_sent = send_part(*two_pair, *ff_pair)
    first_other, hidden_next = after((tp_swap(first_part), hidden_next, ff_sent))[:2]
    ff_part = matmul_nt(hidden_next, ff_weights, 2)
    ff_part_other = tp_swap(ff_part)
    ff_part, second_other = after((ff_part, tp_swap(second_part)))
    grad_resid_low, grad_ff_gain = norm_backward(
        [first_part, first_other, second_part, second_other], None, grad_out, resid, second_scale, ff_gain32
    )
    resid_pair = (grad_resid_low, dp_swap(grad_resid_low))
    grad_attended = dot_nn(grad_resid_low, out_weights_t).astype(bf16)
    down_received, grad_attended = after((y_swap(down_sent), grad_attended))
    down_kept = keep_part(*out_pair, hidden_next, hidden_other, down_received)
    down_done = z_scattered(down_kept)
    grad_attended = after((grad_attended, down_kept))[0]
    grad_query, grad_keys = attention_backward(
        slots,
        rotated,
        keys,
        prompt_mask_t,
        attended,
        inverse,
        grad_attended,
        pairs,
        slot_count,
        prompt_here,
        head_size,
    )
    grad_keys_prompt = grad_keys[:prompt_length].astype(bf16)
    half_prompt = prompt_length // 2
    grad_query_low, query_gain_parts = head_prep_back(
        raw, 0, grad_query, cos_table, sin_table, gains, False, head_size
    )
    query_parts = [
        dot_nt(grad_query_low, qkv_weights[half * half_width : (half + 1) * half_width, :query_width]).astype(bf16)
        for half in range(2)
    ]
    received_keys = y_swap(grad_keys_prompt[half_prompt:])
    query_others = [tp_swap(part) for part in query_parts]
    received_keys, ff_part_other = after((received_keys, ff_part_other, *query_parts))[:2]
    kept_keys = (grad_keys_prompt[:half_prompt].astype(f32) + received_keys.astype(f32)).astype(bf16)
    z_keys = after(
        tuple(z_pass(kept_keys[step * prompt_here : (step + 1) * prompt_here], step) for step in range(1, zsize))
    )
    query_others[0], z_keys = after((query_others[0], z_keys))
    ff_received = after((y_swap(ff_sent), z_keys[0]))[0]
    ff_done = z_scattered(keep_part(*two_pair, *ff_pair, ff_received))
    own_keys = kept_keys[:prompt_here].astype(f32)
    for piece in z_keys:
        own_keys = own_keys + piece.astype(f32)
    grad_key_value = jnp.concatenate([own_keys, grad_keys[prompt_length:]], axis=0)
    out_sent = send_part(*resid_pair, attended, attended_other, zs)
    grad_key_value = after((grad_key_value, out_sent))[0]
    grad_shared_low, key_gain_parts = head_prep_back(
        raw, pairs, grad_key_value, cos_table, sin_table, gains, True, head_size
    )
    grad_shared_other = tp_swap(grad_shared_low)
    grad_qkv = jnp.concatenate([grad_query_low, grad_shared_low], axis=1)
    grad_qkv_other = dp_swap(grad_qkv)
    qkv_sent = send_part(*one_pair, grad_qkv, grad_qkv_other, zs)
    qkv_kept = keep_part(*one_pair, grad_qkv, grad_qkv_other, y_swap(qkv_sent), zs)
    query_others[1], grad_shared_other = after((query_others[1], grad_shared_other, qkv_kept))[:2]
    shared_part = dot_nt(
        jnp.concatenate([grad_shared_low, grad_shared_other], axis=1), shared_weights
    ).astype(bf16)
    grad_input, grad_attn_gain = norm_backward(
        [query_parts[0], query_others[0], query_parts[1], query_others[1]],
        shared_part,
        grad_resid_low,
        inputs_low,
        first_scale,
        attn_gain32,
    )
    qkv_pieces = [z_pass(qkv_kept[step], step) for step in range(1, zsize)]
    out_received, grad_input = after((y_swap(out_sent), grad_input))
    gain_gate, qkv_pieces = after((grad_input, qkv_pieces))
    ff_part, ff_part_other, resid_out = after((ff_part, ff_part_other, resid, grad_input))[:3]
    output = (resid_out.astype(f32) + (ff_part.astype(f32) + ff_part_other.astype(f32))).astype(bf16)
    query_gain_sum = jnp.sum(query_gain_parts.reshape(-1, head_size), axis=0)
    key_gain_sum = jnp.sum(key_gain_parts[:, 0, :head_size], axis=0)
    gain_sums = jnp.concatenate([grad_attn_gain[0], grad_ff_gain[0], query_gain_sum, key_gain_sum]).reshape(-1, lanes)
    gain_sums = gain_sums + dp_swap(gain_sums)
    gain_sums = gain_sums + y_swap(gain_sums)
    out_kept = keep_part(*resid_pair, attended, attended_other, out_received, zs)
    down_done = down_done.astype(f32).T
    gate_done, up_done = split_tiles([ff_done])
    out_done = finish(out_kept).T
    qkv_done = qkv_kept[0].astype(f32)
    for piece in qkv_pieces:
        qkv_done = qkv_done + piece.astype(f32)

    shared_done = qkv_done[:, query_width:]
    shared_other = tp_swap(shared_done)
    from_first = jnp.where(tensor_rank == 0, shared_done, shared_other)
    from_second = jnp.where(tensor_rank == 0, shared_other, shared_done)

    def all_heads(values, offset, which):
        block = values.reshape(-1, slot_count, 2, head_size)[:, :, which].reshape(-1, slot_count * head_size)
        before = offset * head_size
        after = shared_heads * head_size - before - slot_count * head_size
        return jnp.pad(block, ((0, 0), (before, after)))

    key_done, value_done = (
        all_heads(from_first, low_head[0], which) + all_heads(from_second, low_head[1], which)
        for which in range(2)
    )

    gain_total = gain_sums
    for step in range(1, zsize):
        gain_total = gain_total + z_pass(gain_sums, step)
    gain_total = gain_total.reshape(-1)
    head_gains = gain_total[2 * width :]
    head_gains = head_gains + tp_swap(head_gains)
    return (
        output[:prompt_here],
        output[prompt_here:],
        grad_input[:prompt_here],
        grad_input[prompt_here:],
        gain_total[:width],
        qkv_done[:, :query_width],
        key_done,
        value_done,
        head_gains[:head_size],
        head_gains[head_size:],
        out_done,
        gain_total[width : 2 * width],
        gate_done,
        up_done,
        down_done,
    )


def solution(mesh):
    in_specs = (
        P(("dp", "ctx"), None),
        P(("dp", "ctx"), None),
        P(("dp", "ctx")),
        P(),
        P(("dp", "ctx"), "tp"),
        P(("dp", "ctx"), None),
        P(("dp", "ctx"), None),
        P(),
        P(),
        P("tp", ("dp", "ctx")),
        P(),
        P(("dp", "ctx"), "tp"),
        P(("dp", "ctx"), "tp"),
        P("tp", ("dp", "ctx")),
        P(("dp", "ctx"), None),
        P(("dp", "ctx"), None),
    )
    out_specs = (
        P(("dp", "ctx"), None),
        P(("dp", "ctx"), None),
        P(("dp", "ctx"), None),
        P(("dp", "ctx"), None),
        P(),
        P(("dp", "ctx"), "tp"),
        P(("dp", "ctx"), None),
        P(("dp", "ctx"), None),
        P(),
        P(),
        P("tp", ("dp", "ctx")),
        P(),
        P(("dp", "ctx"), "tp"),
        P(("dp", "ctx"), "tp"),
        P("tp", ("dp", "ctx")),
    )
    return jax.shard_map(
        on_device, mesh=mesh, in_specs=in_specs, out_specs=out_specs, check_vma=False
    )
```

```python
from functools import partial

import jax
import jax.numpy as jnp
from jax import lax
from jax.experimental import pallas as pl
from jax.experimental.pallas import tpu as pltpu
from jax.sharding import PartitionSpec as P

epsilon = 1e-06
bf16 = jnp.bfloat16
f32 = jnp.float32
lanes = 128


def params(megabytes=48):
    return pltpu.CompilerParams(vmem_limit_bytes=megabytes << 20)


def cost(flops, bytes_accessed, transcendentals=0, weight=1):
    return pl.CostEstimate(
        flops=int(flops * weight * 0.25),
        bytes_accessed=int(bytes_accessed * weight * 0.25),
        transcendentals=int(transcendentals * weight * 0.25),
    )


def dot_nn(left, right):
    return jnp.dot(left, right, preferred_element_type=f32)


def dot_nt(left, right):
    return lax.dot_general(left, right, (((1,), (1,)), ((), ())), preferred_element_type=f32)


def dot_tn(left, right):
    return lax.dot_general(left, right, (((0,), (0,)), ((), ())), preferred_element_type=f32)


def half_mask(shape, size):
    return lax.broadcasted_iota(jnp.int32, shape, 1) % (2 * size) < size


def swap_quarters(values, head_size):
    quarter = head_size // 2
    low = half_mask(values.shape, quarter)
    return jnp.where(low, pltpu.roll(values, lanes - quarter, 1), pltpu.roll(values, quarter, 1))


def head_sums(values, low):
    first = jnp.sum(jnp.where(low, values, 0.0), axis=1, keepdims=True)
    second = jnp.sum(jnp.where(low, 0.0, values), axis=1, keepdims=True)
    return jnp.where(low, first, second)


def prep_kernel(raw_ref, cos_ref, sin_ref, gain_ref, out_ref, *, query_blocks, head_size, scale):
    block = pl.program_id(0)
    raw = raw_ref[...]
    low = half_mask(raw.shape, head_size)
    inverse = lax.rsqrt(head_sums(raw * raw, low) * (1.0 / head_size) + epsilon)
    normed = raw * inverse * gain_ref[0]
    rotated = normed * cos_ref[...] + swap_quarters(normed, head_size) * sin_ref[...]
    is_query = block < query_blocks
    rotated = rotated * jnp.where(is_query, scale, 1.0)
    out_ref[...] = jnp.where(jnp.logical_or(is_query, low), rotated, raw).astype(bf16)


def head_prep(raw, cos_table, sin_table, gains, query_blocks, head_size, scale):
    rows, width = raw.shape
    return pl.pallas_call(
        partial(prep_kernel, query_blocks=query_blocks, head_size=head_size, scale=scale),
        grid=(width // lanes,),
        in_specs=[
            pl.BlockSpec((rows, lanes), lambda i: (0, i)),
            pl.BlockSpec((rows, lanes), lambda i: (0, 0)),
            pl.BlockSpec((rows, lanes), lambda i: (0, 0)),
            pl.BlockSpec((1, 1, lanes), lambda i: (i, 0, 0)),
        ],
        out_specs=pl.BlockSpec((rows, lanes), lambda i: (0, i)),
        out_shape=jax.ShapeDtypeStruct((rows, width), bf16),
        compiler_params=params(),
        cost_estimate=cost(rows * width * 40, rows * width * 6),
        name="head_prep",
    )(raw, cos_table, sin_table, gains)


def prep_back_kernel(
    raw_ref, grad_ref, cos_ref, sin_ref, gain_ref, out_ref, gain_out_ref, *, has_value, head_size
):
    raw = raw_ref[...]
    grad = grad_ref[...]
    low = half_mask(raw.shape, head_size)
    turned = grad * cos_ref[...] + swap_quarters(grad * sin_ref[...], head_size)
    inverse = lax.rsqrt(head_sums(raw * raw, low) * (1.0 / head_size) + epsilon)
    normed = raw * inverse
    weighted = turned * gain_ref[0]
    mean = head_sums(weighted * normed, low) * (1.0 / head_size)
    result = inverse * (weighted - normed * mean)
    if has_value:
        result = jnp.where(low, result, grad)
    out_ref[...] = result.astype(bf16)
    gain_out_ref[0] = jnp.sum(turned * normed, axis=0, keepdims=True)


def head_prep_back(raw, raw_block, grad, cos_table, sin_table, gains, has_value, head_size):
    rows, width = grad.shape
    blocks = width // lanes
    return pl.pallas_call(
        partial(prep_back_kernel, has_value=has_value, head_size=head_size),
        grid=(blocks,),
        in_specs=[
            pl.BlockSpec((rows, lanes), lambda i: (0, i + raw_block)),
            pl.BlockSpec((rows, lanes), lambda i: (0, i)),
            pl.BlockSpec((rows, lanes), lambda i: (0, 0)),
            pl.BlockSpec((rows, lanes), lambda i: (0, 0)),
            pl.BlockSpec((1, 1, lanes), lambda i: (i + raw_block, 0, 0)),
        ],
        out_specs=[
            pl.BlockSpec((rows, lanes), lambda i: (0, i)),
            pl.BlockSpec((1, 1, lanes), lambda i: (i, 0, 0)),
        ],
        out_shape=[
            jax.ShapeDtypeStruct((rows, width), bf16),
            jax.ShapeDtypeStruct((blocks, 1, lanes), f32),
        ],
        compiler_params=params(),
        cost_estimate=cost(rows * width * 60, rows * width * 10),
        name="head_prep_back",
    )(raw, grad, cos_table, sin_table, gains)


def head_lanes(pair, index, head_size):
    values = pair.astype(f32)
    if index:
        values = pltpu.roll(values, head_size, 1)
    return jnp.where(half_mask(values.shape, head_size), values, 0.0)


def diagonal_mask(keys, rows):
    return lax.broadcasted_iota(jnp.int32, (keys, rows), 0) <= lax.broadcasted_iota(
        jnp.int32, (keys, rows), 1
    )


def attn_fwd_kernel(
    slot_ref, query_ref, keys_ref, mask_ref, out_ref, inverse_ref, acc, *, prompt_here, chunk, head_size
):
    rows = query_ref.shape[0]
    prompt_keys = mask_ref.shape[1]
    cont = rows - prompt_here
    half = cont // 2
    pair = query_ref[...]
    low = half_mask((1, lanes), head_size)
    results = []
    for index in range(2):
        query = head_lanes(pair, index, head_size).astype(bf16)

        def weigh(scores, keyvalue):
            ones_value = jnp.where(low, jnp.ones((), bf16), keyvalue)
            return dot_nn(jnp.exp(scores).astype(bf16), ones_value)

        keyvalue = keys_ref[0:prompt_keys]
        scores = dot_nt(query[:prompt_here], keyvalue)
        weights = (jnp.exp(scores) * mask_ref[...]).astype(bf16)
        acc[0:prompt_here] = dot_nn(weights, jnp.where(low, jnp.ones((), bf16), keyvalue))

        acc[prompt_here:rows] = jnp.zeros((cont, lanes), f32)
        cont_query = query[prompt_here:]

        def prompt_step(step, carry):
            piece = keys_ref[pl.ds(pl.multiple_of(step * chunk, chunk), chunk)]
            acc[prompt_here:rows] += weigh(dot_nt(cont_query, piece), piece)
            return carry

        lax.fori_loop(0, prompt_keys // chunk, prompt_step, 0)
        for block in range(2):
            start = prompt_here + block * half
            piece = keys_ref[prompt_keys + block * half : prompt_keys + (block + 1) * half]
            scores = dot_nt(query[start:], piece)
            row_ids = lax.broadcasted_iota(jnp.int32, scores.shape, 0)
            key_ids = lax.broadcasted_iota(jnp.int32, scores.shape, 1)
            acc[start:rows] += weigh(jnp.where(key_ids <= row_ids, scores, -1e30), piece)
        total = acc[...]
        results.append((total, pltpu.roll(total, head_size, 1)))
    first, first_moved = results[0]
    second, second_moved = results[1]
    full_low = half_mask((rows, lanes), head_size)
    inverse = 1.0 / jnp.where(full_low, first, second_moved)
    inverse_ref[...] = inverse
    out_ref[...] = (jnp.where(full_low, first_moved, second) * inverse).astype(bf16)


def attention_forward(slots, rotated, keys, prompt_mask, pairs, prompt_here, head_size):
    rows = rotated.shape[0]
    key_count = keys.shape[0]
    prompt_keys = prompt_mask.shape[1]
    chunk = min(512, prompt_keys)
    elements = 2 * pairs * rows * key_count
    return pl.pallas_call(
        partial(attn_fwd_kernel, prompt_here=prompt_here, chunk=chunk, head_size=head_size),
        grid_spec=pltpu.PrefetchScalarGridSpec(
            num_scalar_prefetch=1,
            grid=(pairs,),
            in_specs=[
                pl.BlockSpec((rows, lanes), lambda p, s: (0, p)),
                pl.BlockSpec((key_count, lanes), lambda p, s: (0, s[p])),
                pl.BlockSpec(prompt_mask.shape, lambda p, s: (0, 0)),
            ],
            out_specs=[
                pl.BlockSpec((rows, lanes), lambda p, s: (0, p)),
                pl.BlockSpec((rows, lanes), lambda p, s: (0, p)),
            ],
            scratch_shapes=[pltpu.VMEM((rows, lanes), f32)],
        ),
        out_shape=[
            jax.ShapeDtypeStruct((rows, pairs * lanes), bf16),
            jax.ShapeDtypeStruct((rows, pairs * lanes), f32),
        ],
        compiler_params=params(),
        cost_estimate=cost(elements * 1000, elements, elements),
        name="attention_forward",
    )(slots, rotated, keys, prompt_mask)


def attn_back_kernel(
    slot_ref,
    query_ref,
    keys_ref,
    mask_ref,
    attended_ref,
    inverse_ref,
    grad_ref,
    grad_query_ref,
    grad_keys_ref,
    q_sc,
    g_sc,
    d_sc,
    dq_sc,
    *,
    prompt_here,
    chunk,
    head_size,
):
    step_id = pl.program_id(0)
    rows = query_ref.shape[0]
    prompt_keys = mask_ref.shape[0]
    cont = rows - prompt_here
    half = cont // 2
    low = half_mask((1, lanes), head_size)
    full_low = half_mask((rows, lanes), head_size)
    lane_ids = lax.broadcasted_iota(jnp.int32, (rows, lanes), 1)

    fresh = jnp.logical_or(
        step_id == 0, slot_ref[step_id] != slot_ref[jnp.maximum(step_id - 1, 0)]
    )

    @pl.when(fresh)
    def _():
        grad_keys_ref[...] = jnp.zeros_like(grad_keys_ref)

    pair = query_ref[...]
    grad_pair = grad_ref[...].astype(f32)
    inverse = inverse_ref[...]
    product = grad_pair * attended_ref[...].astype(f32)
    delta = head_sums(product, full_low) * inverse
    scaled = grad_pair * inverse
    for index in range(2):
        grad_high = scaled if index else pltpu.roll(scaled, head_size, 1)
        delta_low = pltpu.roll(delta, head_size, 1) if index else delta
        delta_high_part = delta_low.astype(bf16).astype(f32)
        extra = jnp.where(
            lane_ids == 0, -delta_high_part, jnp.where(lane_ids == 1, delta_high_part - delta_low, 0.0)
        )
        q_sc[index] = head_lanes(pair, index, head_size).astype(bf16)
        g_sc[index] = jnp.where(full_low, 0.0, grad_high).astype(bf16)
        d_sc[index] = jnp.where(full_low, extra, grad_high).astype(bf16)
    dq_sc[...] = jnp.zeros_like(dq_sc)

    def block(key_start, key_size, row_start, row_stop, mask):
        piece = keys_ref[pl.ds(key_start, key_size)]
        ones_value = jnp.where(low, jnp.ones((), bf16), piece)
        count = row_stop - row_start

        def rows_of(ref):
            return jnp.concatenate([ref[0, row_start:row_stop], ref[1, row_start:row_stop]], axis=0)

        query = rows_of(q_sc)
        weights = jnp.exp(dot_nt(piece, query))
        if mask is not None:
            weights = mask(weights)
        grad_scores = (weights * dot_nt(ones_value, rows_of(d_sc))).astype(bf16)
        grad_keys_ref[pl.ds(key_start, key_size)] += dot_nn(grad_scores, query) + dot_nn(
            weights.astype(bf16), rows_of(g_sc)
        )
        grad_query = dot_tn(grad_scores, piece)
        dq_sc[0, row_start:row_stop] += grad_query[:count]
        dq_sc[1, row_start:row_stop] += grad_query[count:]

    def prompt_mask(weights):
        mask = mask_ref[...]
        return weights * jnp.concatenate([mask, mask], axis=1)

    block(0, prompt_keys, 0, prompt_here, prompt_mask)

    def prompt_step(step, carry):
        block(pl.multiple_of(step * chunk, chunk), chunk, prompt_here, rows, None)
        return carry

    lax.fori_loop(0, prompt_keys // chunk, prompt_step, 0)
    for part in range(2):
        start = prompt_here + part * half

        def causal(weights, size=rows - start):
            key_ids = lax.broadcasted_iota(jnp.int32, weights.shape, 0)
            row_ids = lax.broadcasted_iota(jnp.int32, weights.shape, 1)
            row_ids = jnp.where(row_ids < size, row_ids, row_ids - size)
            return jnp.where(key_ids <= row_ids, weights, 0.0)

        block(prompt_keys + part * half, half, start, rows, causal)
    moved = pltpu.roll(dq_sc[1], head_size, 1)
    grad_query_ref[...] = jnp.where(full_low, dq_sc[0], moved) * 0.125


def attention_backward(
    slots, rotated, keys, prompt_mask_t, attended, inverse, grad_attended, pairs, slot_count, prompt_here, head_size
):
    rows = rotated.shape[0]
    key_count = keys.shape[0]
    prompt_keys = prompt_mask_t.shape[0]
    chunk = min(512, prompt_keys)
    elements = 2 * pairs * rows * key_count
    pair_spec = pl.BlockSpec((rows, lanes), lambda p, s: (0, p))
    return pl.pallas_call(
        partial(attn_back_kernel, prompt_here=prompt_here, chunk=chunk, head_size=head_size),
        grid_spec=pltpu.PrefetchScalarGridSpec(
            num_scalar_prefetch=1,
            grid=(pairs,),
            in_specs=[
                pair_spec,
                pl.BlockSpec((key_count, lanes), lambda p, s: (0, s[p])),
                pl.BlockSpec(prompt_mask_t.shape, lambda p, s: (0, 0)),
                pair_spec,
                pair_spec,
                pair_spec,
            ],
            out_specs=[
                pair_spec,
                pl.BlockSpec((key_count, lanes), lambda p, s: (0, s[p])),
            ],
            scratch_shapes=[
                pltpu.VMEM((2, rows, lanes), bf16),
                pltpu.VMEM((2, rows, lanes), bf16),
                pltpu.VMEM((2, rows, lanes), bf16),
                pltpu.VMEM((2, rows, lanes), f32),
            ],
        ),
        out_shape=[
            jax.ShapeDtypeStruct((rows, pairs * lanes), f32),
            jax.ShapeDtypeStruct((key_count, slot_count * lanes), f32),
        ],
        compiler_params=params(),
        cost_estimate=cost(elements * 2500, elements, elements, 1),
        name="attention_backward",
    )(slots, rotated, keys, prompt_mask_t, attended, inverse, grad_attended)


ff_tile = 256


def ff_forward_kernel(rows_ref, weight_ref, hidden_ref, gate_factor_ref, up_factor_ref):
    both = dot_nn(rows_ref[...], weight_ref[...])
    gate, up = both[:, :ff_tile], both[:, ff_tile:]
    sigmoid = 1.0 / (1.0 + jnp.exp(-gate))
    silu = gate * sigmoid
    hidden_ref[...] = (silu * up).astype(bf16)
    gate_factor_ref[...] = (up * sigmoid * (1.0 + gate * (1.0 - sigmoid))).astype(bf16)
    up_factor_ref[...] = silu.astype(bf16)


def ff_forward(rows, weights, units):
    count, depth = rows.shape
    out = pl.BlockSpec((count, ff_tile), lambda j: (0, j))
    return pl.pallas_call(
        ff_forward_kernel,
        grid=(units // ff_tile,),
        in_specs=[
            pl.BlockSpec((count, depth), lambda j: (0, 0)),
            pl.BlockSpec((depth, 2 * ff_tile), lambda j: (0, j)),
        ],
        out_specs=[out, out, out],
        out_shape=[jax.ShapeDtypeStruct((count, units), bf16)] * 3,
        compiler_params=params(),
        cost_estimate=cost(4 * count * depth * units, 4 * depth * units, count * units),
        name="ff_forward",
    )(rows, weights)


def matmul_nt_kernel(left_ref, right_ref, out_ref):
    out_ref[...] = dot_nt(left_ref[...], right_ref[...]).astype(bf16)


def matmul_nt(left, weights, column_block, first=0, wide=None, tile=256):
    count, depth = left.shape
    wide = wide or weights.shape[0]
    return pl.pallas_call(
        matmul_nt_kernel,
        grid=(wide // tile,),
        in_specs=[
            pl.BlockSpec((count, depth), lambda j: (0, 0)),
            pl.BlockSpec((tile, depth), lambda j: (j + first // tile, column_block)),
        ],
        out_specs=pl.BlockSpec((count, tile), lambda j: (0, j)),
        out_shape=jax.ShapeDtypeStruct((count, wide), bf16),
        compiler_params=params(),
        cost_estimate=cost(2 * count * depth * wide, 2 * depth * wide),
        name="matmul_nt",
    )(left, weights)


def split_tiles_kernel(*refs, bounds):
    gate_ref, up_ref = refs[-2:]
    step = pl.program_id(0)
    for part_ref, start, stop in zip(refs, bounds, bounds[1:]):

        @pl.when(jnp.logical_and(step >= start, step < stop))
        def _(part_ref=part_ref):
            gate_ref[...] = part_ref[:, :ff_tile].astype(f32)
            up_ref[...] = part_ref[:, ff_tile:].astype(f32)


def split_tiles(parts):
    rows = parts[0].shape[0]
    bounds = [0]
    for part in parts:
        bounds.append(bounds[-1] + part.shape[1] // (2 * ff_tile))
    out = pl.BlockSpec((rows, ff_tile), lambda j: (0, j))
    in_specs = [
        pl.BlockSpec(
            (rows, 2 * ff_tile),
            lambda j, start=start, stop=stop: (0, jnp.clip(j - start, 0, stop - start - 1)),
        )
        for start, stop in zip(bounds, bounds[1:])
    ]
    return pl.pallas_call(
        partial(split_tiles_kernel, bounds=bounds),
        grid=(bounds[-1],),
        in_specs=in_specs,
        out_specs=[out, out],
        out_shape=[jax.ShapeDtypeStruct((rows, bounds[-1] * ff_tile), f32)] * 2,
        compiler_params=params(),
        cost_estimate=cost(0, rows * bounds[-1] * ff_tile * 12),
        name="split_tiles",
    )(*parts)


def norm_back_kernel(*refs, halves, extra):
    addends, refs = refs[: 2 * halves], refs[2 * halves :]
    grad = jnp.concatenate(
        [addends[2 * half][...].astype(f32) + addends[2 * half + 1][...].astype(f32) for half in range(halves)],
        axis=1,
    )
    if extra:
        grad, refs = grad + refs[0][...].astype(f32), refs[1:]
    base_ref, values_ref, scale_ref, gain_ref, out_ref, gain_grad_ref = refs
    scale = scale_ref[...]
    normed = values_ref[...].astype(f32) * scale
    weighted = grad * gain_ref[...]
    mean = jnp.mean(weighted * normed, axis=-1, keepdims=True)

    @pl.when(pl.program_id(0) == 0)
    def _():
        gain_grad_ref[...] = jnp.zeros_like(gain_grad_ref)

    gain_grad_ref[...] += jnp.sum(grad * normed, axis=0, keepdims=True)
    out_ref[...] = (base_ref[...].astype(f32) + scale * (weighted - normed * mean)).astype(bf16)


def norm_backward(addends, extra, base, values, scale, gain, tile=128):
    rows, width = base.shape
    row_spec = pl.BlockSpec((tile, width), lambda i: (i, 0))
    one_spec = pl.BlockSpec((1, width), lambda i: (0, 0))
    half_spec = pl.BlockSpec((tile, addends[0].shape[1]), lambda i: (i, 0))
    operands = list(addends) + ([extra] if extra is not None else []) + [base, values, scale, gain[None]]
    in_specs = [half_spec] * len(addends) + [row_spec] * (3 if extra is not None else 2)
    in_specs += [pl.BlockSpec((tile, 1), lambda i: (i, 0)), one_spec]
    return pl.pallas_call(
        partial(norm_back_kernel, halves=len(addends) // 2, extra=extra is not None),
        grid=(rows // tile,),
        in_specs=in_specs,
        out_specs=[row_spec, one_spec],
        out_shape=[jax.ShapeDtypeStruct((rows, width), bf16), jax.ShapeDtypeStruct((1, width), f32)],
        compiler_params=params(),
        cost_estimate=cost(rows * width * 20, rows * width * 12),
        name="norm_backward",
    )(*operands)


def ff_back_kernel(grad_ref, weight_ref, gate_factor_ref, up_factor_ref, out_ref):
    grad_hidden = dot_nn(grad_ref[...], weight_ref[...])
    out_ref[:, :ff_tile] = (grad_hidden * gate_factor_ref[...].astype(f32)).astype(bf16)
    out_ref[:, ff_tile:] = (grad_hidden * up_factor_ref[...].astype(f32)).astype(bf16)


def ff_backward(grad_out, weights, gate_factor, up_factor):
    count, depth = grad_out.shape
    units = gate_factor.shape[1]
    tiles = units // ff_tile
    factor = pl.BlockSpec((count, ff_tile), lambda j: (0, j))
    return pl.pallas_call(
        ff_back_kernel,
        grid=(tiles,),
        in_specs=[
            pl.BlockSpec((count, depth), lambda j: (0, 0)),
            pl.BlockSpec((depth, ff_tile), lambda j: (0, j + 2 * tiles)),
            factor,
            factor,
        ],
        out_specs=pl.BlockSpec((count, 2 * ff_tile), lambda j: (0, j)),
        out_shape=jax.ShapeDtypeStruct((count, 2 * units), bf16),
        compiler_params=params(),
        cost_estimate=cost(2 * count * depth * units, 2 * depth * units),
        name="ff_backward",
    )(grad_out, weights, gate_factor, up_factor)


def weight_grad_kernel(index_ref, left_own_ref, left_other_ref, own_ref, other_ref, *rest, pieces, block):
    out_ref, left_t = rest[-2:]
    rows = own_ref.shape[0]

    @pl.when(pl.program_id(0) == 0)
    def _():
        left_t[:, :rows] = left_own_ref[...].T
        left_t[:, rows:] = left_other_ref[...].T

    left = jnp.concatenate(
        [left_t[pl.ds(pl.multiple_of(index_ref[piece] * block, block), block)] for piece in range(pieces)],
        axis=0,
    )
    right = jnp.concatenate([own_ref[...], other_ref[...]], axis=0)
    product = dot_nn(left, right)
    for piece in range(pieces):
        part = product[piece * block : (piece + 1) * block]
        if len(rest) == 3:
            part = part + rest[0][piece].astype(f32)
        out_ref[piece] = part.astype(bf16)


def weight_grad(indices, rank, block, left, left_other, own, other, received=None, first=0, wide=None):
    pieces = indices.shape[0]
    rows = own.shape[0]
    wide = wide or own.shape[1]
    half = left.shape[1] // 2
    tile = next(size for size in (640, 512, 384, lanes) if wide % size == 0 and first % size == 0)
    out = pl.BlockSpec((pieces, block, tile), lambda j, s: (0, 0, j))
    left_spec = pl.BlockSpec((rows, half), lambda j, s: (0, s[pieces]))
    in_specs = [left_spec] * 2 + [pl.BlockSpec((rows, tile), lambda j, s: (0, j + first // tile))] * 2
    operands = [left, left_other, own, other]
    if received is not None:
        in_specs.append(pl.BlockSpec((pieces, block, tile), lambda j, s: (0, 0, j)))
        operands.append(received)
    return pl.pallas_call(
        partial(weight_grad_kernel, pieces=pieces, block=block),
        grid_spec=pltpu.PrefetchScalarGridSpec(
            num_scalar_prefetch=1,
            grid=(wide // tile,),
            in_specs=in_specs,
            out_specs=out,
            scratch_shapes=[pltpu.VMEM((half, 2 * rows), bf16)],
        ),
        out_shape=jax.ShapeDtypeStruct((pieces, block, wide), bf16),
        compiler_params=params(),
        cost_estimate=cost(4 * pieces * block * rows * wide, 2 * (pieces * block + 2 * rows) * wide),
        name="weight_grad",
    )(jnp.concatenate([indices, rank[None]]), *operands)


def gather_blocks_kernel(place_ref, *refs):
    count = (len(refs) - 2) // 1
    out_ref, sems = refs[-2:]
    copies = [
        pltpu.make_async_copy(refs[i], out_ref.at[place_ref[i]], sems.at[i]) for i in range(count)
    ]
    for copy in copies:
        copy.start()
    for copy in copies:
        copy.wait()


def gather_blocks(places, blocks):
    count = len(blocks)
    any_spec = pl.BlockSpec(memory_space=pl.ANY)
    return pl.pallas_call(
        gather_blocks_kernel,
        grid_spec=pltpu.PrefetchScalarGridSpec(
            num_scalar_prefetch=1,
            grid=(1,),
            in_specs=[any_spec] * count,
            out_specs=any_spec,
            scratch_shapes=[pltpu.SemaphoreType.DMA((count,))],
        ),
        out_shape=jax.ShapeDtypeStruct((count,) + blocks[0].shape, blocks[0].dtype),
        cost_estimate=cost(0, 2 * count * blocks[0].size * 2),
        name="gather_blocks",
    )(places, *blocks)


def after(values):
    return lax.optimization_barrier(values)


def on_device(
    prompt_states,
    continuation_states,
    continuation_offset,
    attention_gain,
    query_weight,
    key_weight,
    value_weight,
    query_gain,
    key_gain,
    output_weight,
    feedforward_gain,
    gate_weight,
    up_weight,
    down_weight,
    grad_prompt,
    grad_continuation,
):
    ring = lax.axis_size("ctx")
    tensor_size = lax.axis_size("tp")
    zsize, ysize = ring // 2, 2
    prompt_here, width = prompt_states.shape
    cont_length = continuation_states.shape[0]
    rows_here = prompt_here + cont_length
    prompt_length = prompt_here * ring
    head_size = query_gain.shape[0]
    query_width = query_weight.shape[1]
    local_heads = query_width // head_size
    shared_heads = key_weight.shape[1] // head_size
    group_size = local_heads * tensor_size // shared_heads
    pairs = local_heads // 2
    units = gate_weight.shape[1]
    half_width = width // 2
    block = half_width // ring
    low_head = [t * local_heads // group_size for t in range(tensor_size)]
    slot_count = max(
        ((t + 1) * local_heads - 1) // group_size - low_head[t] + 1 for t in range(tensor_size)
    )

    data_rank = lax.axis_index("dp")
    context_rank = lax.axis_index("ctx")
    tensor_rank = lax.axis_index("tp")
    zrank, yrank = context_rank // ysize, context_rank % ysize
    first_shared = tensor_rank * local_heads // group_size

    def z_pass(values, shift):
        pairs_of = [
            (z * ysize + y, (z + shift) % zsize * ysize + y) for z in range(zsize) for y in range(ysize)
        ]
        return lax.ppermute(values, "ctx", pairs_of)

    def y_swap(values):
        return lax.ppermute(values, "ctx", [(i, i ^ 1) for i in range(ring)])

    def dp_swap(values):
        return lax.ppermute(values, "dp", [(0, 1), (1, 0)])

    def tp_swap(values):
        return lax.ppermute(values, "tp", [(0, 1), (1, 0)])

    def shared_slots(weight):
        return lax.dynamic_slice_in_dim(weight, first_shared * head_size, slot_count * head_size, 1).reshape(
            -1, slot_count, head_size
        )

    def interleaved(gate, up):
        tiles = units // ff_tile
        both = jnp.stack([gate.reshape(-1, tiles, ff_tile), up.reshape(-1, tiles, ff_tile)], axis=2)
        return both.reshape(-1, 2 * units)

    key_value_weight = jnp.concatenate(
        [shared_slots(key_weight), shared_slots(value_weight)], axis=2
    ).reshape(-1, slot_count * lanes)
    qkv_width = query_width + slot_count * lanes
    attn_weights = lax.all_gather(
        jnp.concatenate([query_weight, key_value_weight, output_weight.T], axis=1),
        ("dp", "ctx"),
        axis=0,
        tiled=True,
    )
    ff_weights = lax.all_gather(
        jnp.concatenate([interleaved(gate_weight, up_weight), down_weight.T], axis=1),
        ("dp", "ctx"),
        axis=0,
        tiled=True,
    )
    qkv_weights = attn_weights[:, :qkv_width]
    shared_weights = attn_weights[:, query_width:qkv_width]
    out_weights_t = attn_weights[:, qkv_width:]

    row_ids = jnp.arange(rows_here, dtype=jnp.int32)
    positions = jnp.where(
        row_ids < prompt_here,
        context_rank * prompt_here + row_ids,
        prompt_length + continuation_offset[0] + row_ids - prompt_here,
    ).astype(f32)
    freqs = 10000.0 ** (-(2.0 * jnp.arange(head_size // 2, dtype=f32)) / head_size)
    angles = positions[:, None] * freqs[None, :]
    cosine, sine = jnp.cos(angles), jnp.sin(angles)
    cos_table = jnp.concatenate([cosine] * 4, axis=1)
    sin_table = jnp.concatenate([-sine, sine] * 2, axis=1)
    query_gain32, key_gain32 = query_gain.astype(f32), key_gain.astype(f32)
    gains = jnp.concatenate(
        [
            jnp.broadcast_to(jnp.concatenate([query_gain32] * 2), (pairs, 1, lanes)),
            jnp.broadcast_to(
                jnp.concatenate([key_gain32, jnp.ones((head_size,), f32)]), (slot_count, 1, lanes)
            ),
        ],
        axis=0,
    )
    steps = jnp.arange(zsize, dtype=jnp.int32)
    zs = (zrank + steps) % zsize
    own_blocks = zs * ysize + yrank
    other_blocks = zs * ysize + (1 - yrank)
    chunk_order = jnp.concatenate([own_blocks, other_blocks])
    key_places = jnp.repeat(chunk_order * prompt_here, prompt_here) + jnp.tile(
        jnp.arange(prompt_here, dtype=jnp.int32), ring
    )
    query_places = context_rank * prompt_here + jnp.arange(prompt_here, dtype=jnp.int32)
    prompt_mask = (key_places[None, :] <= query_places[:, None]).astype(f32)
    prompt_mask_t = (key_places[:, None] <= query_places[None, :]).astype(f32)
    slots = (
        (tensor_rank * local_heads + 2 * jnp.arange(pairs, dtype=jnp.int32)) // group_size - first_shared
    ).astype(jnp.int32)

    inputs_low = jnp.concatenate([prompt_states, continuation_states], axis=0)
    inputs = inputs_low.astype(f32)
    attn_gain32 = attention_gain.astype(f32)
    ff_gain32 = feedforward_gain.astype(f32)
    first_scale = lax.rsqrt(jnp.mean(inputs * inputs, axis=-1, keepdims=True) + epsilon)
    normed_low = (inputs * first_scale * attn_gain32).astype(bf16)
    raw = dot_nn(normed_low, qkv_weights)
    rotated = head_prep(raw, cos_table, sin_table, gains, pairs, head_size, 0.125)
    key_value = rotated[:, query_width:]
    own_chunk = key_value[:prompt_here]
    z_chunks = [own_chunk] + [z_pass(own_chunk, zsize - step) for step in range(1, zsize)]
    z_part = jnp.concatenate(z_chunks, axis=0)
    keys = jnp.concatenate([z_part, y_swap(z_part), key_value[prompt_here:]], axis=0)
    attended, inverse = attention_forward(
        slots, rotated, keys, prompt_mask, pairs, prompt_here, head_size
    )
    shared_weights = jnp.concatenate([shared_weights, tp_swap(shared_weights)], axis=1)
    attended, shared_weights = after((attended, shared_weights))
    attn_part = dot_nt(attended, out_weights_t).astype(bf16)
    resid32 = inputs + (attn_part.astype(f32) + tp_swap(attn_part).astype(f32))
    resid = resid32.astype(bf16)
    second_scale = lax.rsqrt(jnp.mean(resid32 * resid32, axis=-1, keepdims=True) + epsilon)
    normed_two = (resid32 * second_scale * ff_gain32).astype(bf16)
    grad_out = jnp.concatenate([grad_prompt, grad_continuation], axis=0)
    normed_two, two_other, out_other, one_other, attended_other = after(
        (normed_two, dp_swap(normed_two), dp_swap(grad_out), dp_swap(normed_low), dp_swap(attended))
    )
    hidden, gate_factor, up_factor = ff_forward(normed_two, ff_weights, units)

    def send_part(left, left_other, own, other, order=None, **span):
        indices = (steps if order is None else order) * ysize + 1 - yrank
        return weight_grad(indices, data_rank, block, left, left_other, own, other, **span)

    def keep_part(left, left_other, own, other, received, order=None, **span):
        indices = (steps if order is None else order) * ysize + yrank
        return weight_grad(indices, data_rank, block, left, left_other, own, other, received, **span)

    z_groups = [[z * ysize + y for z in range(zsize)] for y in range(ysize)]

    def z_scattered(kept):
        scattered = lax.psum_scatter(
            kept, "ctx", scatter_dimension=0, axis_index_groups=z_groups, tiled=True
        )
        return scattered[0]

    def finish(kept):
        total = kept[0].astype(f32)
        for step in range(1, zsize):
            total = total + z_pass(kept[step], step).astype(f32)
        return total

    out_pair, two_pair, one_pair = (grad_out, out_other), (normed_two, two_other), (normed_low, one_other)

    grad_ff = ff_backward(grad_out, ff_weights, gate_factor, up_factor)
    hidden_other, grad_ff = after((dp_swap(hidden), grad_ff))
    grad_ff_other = dp_swap(grad_ff)
    down_sent = send_part(*out_pair, hidden, hidden_other)
    hidden, grad_ff, down_sent = after((hidden, grad_ff, down_sent))
    first_part = matmul_nt(grad_ff, ff_weights, 0, 0, half_width)
    grad_ff, first_part = after((grad_ff, first_part))
    second_part = matmul_nt(grad_ff, ff_weights, 0, half_width, half_width)
    grad_ff, hidden_next, second_part = after((grad_ff, hidden, second_part))
    ff_pair = (grad_ff, grad_ff_other)
    ff_sent = send_part(*two_pair, *ff_pair)
    first_other, hidden_next = after((tp_swap(first_part), hidden_next, ff_sent))[:2]
    ff_part = matmul_nt(hidden_next, ff_weights, 2)
    ff_part_other = tp_swap(ff_part)
    ff_part, second_other = after((ff_part, tp_swap(second_part)))
    grad_resid_low, grad_ff_gain = norm_backward(
        [first_part, first_other, second_part, second_other], None, grad_out, resid, second_scale, ff_gain32
    )
    resid_pair = (grad_resid_low, dp_swap(grad_resid_low))
    grad_attended = dot_nn(grad_resid_low, out_weights_t).astype(bf16)
    down_received, grad_attended = after((y_swap(down_sent), grad_attended))
    down_kept = keep_part(*out_pair, hidden_next, hidden_other, down_received)
    down_done = z_scattered(down_kept)
    grad_attended = after((grad_attended, down_kept))[0]
    grad_query, grad_keys = attention_backward(
        slots,
        rotated,
        keys,
        prompt_mask_t,
        attended,
        inverse,
        grad_attended,
        pairs,
        slot_count,
        prompt_here,
        head_size,
    )
    grad_keys_prompt = grad_keys[:prompt_length].astype(bf16)
    half_prompt = prompt_length // 2
    grad_query_low, query_gain_parts = head_prep_back(
        raw, 0, grad_query, cos_table, sin_table, gains, False, head_size
    )
    query_parts = [
        dot_nt(grad_query_low, qkv_weights[half * half_width : (half + 1) * half_width, :query_width]).astype(bf16)
        for half in range(2)
    ]
    received_keys = y_swap(grad_keys_prompt[half_prompt:])
    query_others = [tp_swap(part) for part in query_parts]
    received_keys, ff_part_other = after((received_keys, ff_part_other, *query_parts))[:2]
    kept_keys = (grad_keys_prompt[:half_prompt].astype(f32) + received_keys.astype(f32)).astype(bf16)
    z_keys = after(
        tuple(z_pass(kept_keys[step * prompt_here : (step + 1) * prompt_here], step) for step in range(1, zsize))
    )
    query_others[0], z_keys = after((query_others[0], z_keys))
    ff_received = after((y_swap(ff_sent), z_keys[0]))[0]
    ff_done = z_scattered(keep_part(*two_pair, *ff_pair, ff_received))
    own_keys = kept_keys[:prompt_here].astype(f32)
    for piece in z_keys:
        own_keys = own_keys + piece.astype(f32)
    grad_key_value = jnp.concatenate([own_keys, grad_keys[prompt_length:]], axis=0)
    out_sent = send_part(*resid_pair, attended, attended_other, zs)
    grad_key_value = after((grad_key_value, out_sent))[0]
    grad_shared_low, key_gain_parts = head_prep_back(
        raw, pairs, grad_key_value, cos_table, sin_table, gains, True, head_size
    )
    grad_shared_other = tp_swap(grad_shared_low)
    grad_qkv = jnp.concatenate([grad_query_low, grad_shared_low], axis=1)
    grad_qkv_other = dp_swap(grad_qkv)
    qkv_sent = send_part(*one_pair, grad_qkv, grad_qkv_other, zs)
    qkv_kept = keep_part(*one_pair, grad_qkv, grad_qkv_other, y_swap(qkv_sent), zs)
    query_others[1], grad_shared_other = after((query_others[1], grad_shared_other, qkv_kept))[:2]
    shared_part = dot_nt(
        jnp.concatenate([grad_shared_low, grad_shared_other], axis=1), shared_weights
    ).astype(bf16)
    grad_input, grad_attn_gain = norm_backward(
        [query_parts[0], query_others[0], query_parts[1], query_others[1]],
        shared_part,
        grad_resid_low,
        inputs_low,
        first_scale,
        attn_gain32,
    )
    qkv_pieces = [z_pass(qkv_kept[step], step) for step in range(1, zsize)]
    out_received, grad_input = after((y_swap(out_sent), grad_input))
    out_received, qkv_pieces = after((out_received, qkv_pieces))
    ff_part, ff_part_other, resid_out = after((ff_part, ff_part_other, resid, grad_input))[:3]
    output = (resid_out.astype(f32) + (ff_part.astype(f32) + ff_part_other.astype(f32))).astype(bf16)
    query_gain_sum = jnp.sum(query_gain_parts.reshape(-1, head_size), axis=0)
    key_gain_sum = jnp.sum(key_gain_parts[:, 0, :head_size], axis=0)
    gain_sums = jnp.concatenate([grad_attn_gain[0], grad_ff_gain[0], query_gain_sum, key_gain_sum]).reshape(-1, lanes)
    gain_sums = gain_sums + dp_swap(gain_sums)
    gain_sums = gain_sums + y_swap(gain_sums)
    out_kept = keep_part(*resid_pair, attended, attended_other, out_received, zs)
    down_done = down_done.astype(f32).T
    gate_done, up_done = split_tiles([ff_done])
    out_done = finish(out_kept).T
    qkv_done = qkv_kept[0].astype(f32)
    for piece in qkv_pieces:
        qkv_done = qkv_done + piece.astype(f32)

    shared_done = qkv_done[:, query_width:]
    shared_other = tp_swap(shared_done)
    from_first = jnp.where(tensor_rank == 0, shared_done, shared_other)
    from_second = jnp.where(tensor_rank == 0, shared_other, shared_done)

    def all_heads(values, offset, which):
        block = values.reshape(-1, slot_count, 2, head_size)[:, :, which].reshape(-1, slot_count * head_size)
        before = offset * head_size
        after = shared_heads * head_size - before - slot_count * head_size
        return jnp.pad(block, ((0, 0), (before, after)))

    key_done, value_done = (
        all_heads(from_first, low_head[0], which) + all_heads(from_second, low_head[1], which)
        for which in range(2)
    )

    gain_total = gain_sums
    for step in range(1, zsize):
        gain_total = gain_total + z_pass(gain_sums, step)
    gain_total = gain_total.reshape(-1)
    head_gains = gain_total[2 * width :]
    head_gains = head_gains + tp_swap(head_gains)
    return (
        output[:prompt_here],
        output[prompt_here:],
        grad_input[:prompt_here],
        grad_input[prompt_here:],
        gain_total[:width],
        qkv_done[:, :query_width],
        key_done,
        value_done,
        head_gains[:head_size],
        head_gains[head_size:],
        out_done,
        gain_total[width : 2 * width],
        gate_done,
        up_done,
        down_done,
    )


def solution(mesh):
    in_specs = (
        P(("dp", "ctx"), None),
        P(("dp", "ctx"), None),
        P(("dp", "ctx")),
        P(),
        P(("dp", "ctx"), "tp"),
        P(("dp", "ctx"), None),
        P(("dp", "ctx"), None),
        P(),
        P(),
        P("tp", ("dp", "ctx")),
        P(),
        P(("dp", "ctx"), "tp"),
        P(("dp", "ctx"), "tp"),
        P("tp", ("dp", "ctx")),
        P(("dp", "ctx"), None),
        P(("dp", "ctx"), None),
    )
    out_specs = (
        P(("dp", "ctx"), None),
        P(("dp", "ctx"), None),
        P(("dp", "ctx"), None),
        P(("dp", "ctx"), None),
        P(),
        P(("dp", "ctx"), "tp"),
        P(("dp", "ctx"), None),
        P(("dp", "ctx"), None),
        P(),
        P(),
        P("tp", ("dp", "ctx")),
        P(),
        P(("dp", "ctx"), "tp"),
        P(("dp", "ctx"), "tp"),
        P("tp", ("dp", "ctx")),
    )
    return jax.shard_map(
        on_device, mesh=mesh, in_specs=in_specs, out_specs=out_specs, check_vma=False
    )
```
